32 devices in a mesh: group: 2 (over y), section: 4 (over z), seq: 2 (over x), tp: 2 (over core).
Axes of the slice: x: 2, y: 2, z: 4, core: 2. Of those that a mesh axis runs over, the one named last changes fastest.
Arguments:
- handoff: bfloat16 [8, 768, 8192], P(('group', 'section'), 'seq', 'tp'), parts along dimension 0, may hold values from -6 to 6
- norm_gain: float32 [4, 8192], P('section'), may hold values from 0.5 to 1.5
- kv_weight: bfloat16 [4, 8192, 4, 256], P('section', 'seq', 'tp'), may hold values from -0.0625 to 0.0625
- span_start: int32 [8], P(('group', 'section')), parts along dimension 0, may hold values from 0 to 4095
- token_owner: int32 [8, 768, 1], P(('group', 'section'), 'seq'), parts along dimension 0, may hold values from 0 to 3; in each aligned block of 384 rows (0 to 383, 384 to 767, ..., all dimensions but the last counted through in order) at most 192 rows name the same one
- token_slot: int32 [8, 768], P(('group', 'section'), 'seq'), parts along dimension 0, may hold values from 0 to 1
- kv_cache: bfloat16 [8, 2, 4, 2, 32, 4, 256], P(('group', 'section'), 'seq', None, None, None, 'tp'), parts along dimension 0, may hold values from -4 to 4
- cache_lens: int32 [8, 2, 2], P(('group', 'section'), 'seq'), parts along dimension 0, may hold values from 2 to 32
- step_kv: bfloat16 [8, 2, 4, 2, 2, 4, 256], P(('group', 'section'), 'seq', None, None, None, 'tp'), parts along dimension 0, may hold values from -6 to 6
- queries: bfloat16 [8, 2, 4, 2, 2, 4, 1024], P(('group', 'section'), 'seq', None, None, None, 'tp'), parts along dimension 0, may hold values from -80 to 80
Outputs:
- decode_out: bfloat16 [8, 2, 4, 2, 2, 4, 1024], P(('group', 'section'), 'seq', None, None, None, 'tp'), parts along dimension 0
The draws below stay inside these ranges and needn't reach their ends.
There are 2 independent parts, one for each index of `group`. The reference program is written for one: setup_inputs(seed, part) draws one part's arguments, and reference() takes and returns one part's arrays. A program takes and returns all parts, laid end to end along the dimension named above; an argument that names none is the same for every part. Nothing has to cross between parts.
Inputs may be any that keep to these rules, and one draw needn't show every extreme that they name: `token_owner`: among the 384 tokens of one device's rows (aligned blocks), no owner section is named by more than 192 tokens.
All inputs are finite; a program needn't handle non-finite values.
Results may differ from the reference program's by a relative error of at most 0.0066.
Values may be sent and summed in bfloat16 or wider, within the bound.
No kernel may reach another device: no remote copies, remote signals or barrier semaphores. Data moves between devices by JAX's collectives and lax.ppermute only.
A program may use at most 128 MiB of HBM per device.

```python
import math
import jax
import jax.numpy as jnp
import numpy as np
from jax import lax

D = 8192
HD = 128
GQ = 8
KVH = 4
TOK_DEV = 384
REQ_DEV = 2
CACHE = 32
STEPS = 2
LAYERS = 4
SPAN = 768
CAP = 192
N_SECTION = 4
N_SEQ = 2


def stored_pairs(key):
    shape = (N_SECTION, N_SEQ, LAYERS, REQ_DEV, CACHE, KVH, 2 * HD)
    return jnp.clip(jax.random.normal(jax.random.fold_in(key, 7), shape, jnp.float32), -4.0, 4.0)


def draw_kv_cache(key, part):
    stored = stored_pairs(key)
    return stored.astype(jnp.bfloat16)


def draw_queries(key, part):
    shape = (N_SECTION, N_SEQ, LAYERS, REQ_DEV, STEPS, KVH, GQ, HD)
    drawn = jnp.clip(jax.random.normal(jax.random.fold_in(key, 9), shape, jnp.float32), -6.0, 6.0)
    return drawn.reshape(N_SECTION, N_SEQ, LAYERS, REQ_DEV, STEPS, KVH, GQ * HD).astype(jnp.bfloat16)


def plant(values, rng, smallest, largest):
    spot = [jax.random.randint(jax.random.fold_in(rng, axis), (), 0, length) for axis, length in enumerate(values.shape)]
    main_axis = values.shape.index(max(values.shape))
    beside = spot[:main_axis] + [(spot[main_axis] + 1) % values.shape[main_axis]] + spot[main_axis + 1:]
    return values.at[tuple(spot)].set(smallest).at[tuple(beside)].set(largest)


def levels(key, dims, pieces, least, high):
    def one(position, blocks):
        draws = jax.random.uniform(jax.random.fold_in(jax.random.fold_in(key, 6), position), (blocks,), jnp.float32, least / len(pieces), high / len(pieces))
        return jnp.repeat(jnp.exp(draws), dims[position] // blocks).reshape((-1,) + (1,) * (len(dims) - position - 1))

    factor_of = one(*pieces[0])
    for cut in pieces[1:]:
        factor_of = factor_of * one(*cut)
    return factor_of


def shared_out(own_key, own, number, rows, number_of, top, most, skew):
    order = jax.random.permutation(own_key, number_of)
    packed, usual = portions_of(number_of, rows * top, most, skew, True), portions_of(number_of, rows * top, most, skew, False)
    places = jnp.arange(number_of)

    def named(sizes, turn):
        used = int((sizes > 0).sum())
        fixed = max(1, used // 4)
        shifted = fixed + (places - fixed + turn * (used - fixed)) % max(1, number_of - fixed)
        return jnp.zeros((number_of,), jnp.int32).at[order[jnp.where(places < fixed, places, shifted)]].set(jnp.asarray(sizes, jnp.int32))

    sizes = jnp.where(number % 4 == 0, named(packed, number // 4), named(usual, number - number // 4 - 1))
    mixed = jax.random.permutation(jax.random.fold_in(own, 3), number_of)
    donor, receiver = mixed[0:number_of // 2 * 2:2], mixed[1:number_of // 2 * 2:2]
    margin = jnp.minimum(sizes[donor] - 1, most - sizes[receiver]) // 2
    margin = jnp.where((donor == order[0]) | (receiver == order[0]) | (sizes[receiver] == 0), 0, jnp.maximum(margin, 0))
    shifted = jax.random.randint(jax.random.fold_in(own, 4), (number_of // 2,), 0, 1 << 20) % (margin + 1)
    sizes = sizes.at[donor].add(-shifted).at[receiver].add(shifted)
    labels = jnp.searchsorted(jnp.cumsum(sizes), jnp.arange(rows * top), side="right").astype(jnp.int32)
    listing = labels.reshape(top, rows).T
    listing = listing[jax.random.permutation(jax.random.fold_in(own, 1), rows)]
    turn = jax.random.randint(jax.random.fold_in(own, 2), (rows, 1), 0, top)
    return jnp.take_along_axis(listing, (jnp.arange(top)[None, :] + turn) % top, axis=1)


def portions_of(number_of, total, reach, lean, full):
    portions = [(1 << 20) // math.isqrt(standing ** lean) + 1 for standing in range(1, number_of + 1)]
    largest = reach if full else min(reach, max(-(-total // number_of), total * portions[0] // sum(portions)))
    least = 1 if total - largest >= number_of - 1 else 0
    holding, rest = [largest] + [least] * (number_of - 1), total - largest - least * (number_of - 1)
    while rest > 0:
        candidates = [i for i in range(1, number_of) if holding[i] < largest] or [i for i in range(1, number_of) if holding[i] < reach]
        pool, left = sum([portions[i] for i in candidates]), rest
        for i in candidates:
            addition = min(reach - holding[i], max(1, left * portions[i] // pool), rest)
            holding[i] = holding[i] + addition
            rest = rest - addition
    return np.array(holding)


def noise(stream_key, shape, scale, reach, split=(), held_as=jnp.bfloat16):
    array = scale * jax.random.normal(stream_key, shape, jnp.float32)
    if split:
        array = array * levels(stream_key, shape, split, -0.22, 0.18)
    return jnp.clip(array, -reach, reach).astype(held_as)


def setup_inputs(seed: int = 0, part: int = 0) -> dict:
    streams_of = jax.random.split(jax.random.key(seed), 11)
    part_keys = jax.random.split(jax.random.fold_in(streams_of[10], part), 11)
    handoff = noise(part_keys[0], (LAYERS, SPAN, D), 1.0, 6.0, ((0, 4), (1, 2), (2, 2)))
    norm_gain = jnp.clip(0.5 + 1.0 * jax.random.uniform(streams_of[1], (LAYERS, D), jnp.float32) ** levels(streams_of[1], (LAYERS, D), ((0, 4),), -0.2, 0.2), 0.5, 1.5)
    kv_weight = noise(streams_of[2], (LAYERS, D, KVH, 2 * HD), D ** -0.5, 0.0625, ((0, 4), (1, 2), (2, 2)))
    span_start = plant(jax.random.randint(part_keys[3], (LAYERS,), 0, 4096), jax.random.fold_in(part_keys[3], 1), 0, 4095).astype(jnp.int32)
    token_owner_keys = jax.random.split(jax.random.fold_in(part_keys[4], 1), LAYERS * SPAN // TOK_DEV)
    token_owner_turns = jax.random.permutation(jax.random.fold_in(part_keys[4], 3), LAYERS * SPAN // TOK_DEV)
    token_owner = jax.vmap(lambda own, number: shared_out(jax.random.fold_in(part_keys[4], 2), own, number, TOK_DEV, N_SECTION, 1, CAP, 2))(token_owner_keys, token_owner_turns).reshape((LAYERS, SPAN, 1))
    token_slot = plant(jax.random.randint(part_keys[5], (LAYERS, SPAN), 0, REQ_DEV), jax.random.fold_in(part_keys[5], 1), 0, REQ_DEV - 1).astype(jnp.int32)
    kv_cache = draw_kv_cache(jax.random.fold_in(jax.random.fold_in(streams_of[10], part), 71), part)
    cache_lens = plant(jax.random.randint(part_keys[7], (N_SECTION, N_SEQ, REQ_DEV), 2, CACHE + 1), jax.random.fold_in(part_keys[7], 1), 2, CACHE).astype(jnp.int32)
    step_kv = noise(part_keys[8], (N_SECTION, N_SEQ, LAYERS, REQ_DEV, STEPS, KVH, 2 * HD), 1.0, 6.0, ((0, 4), (1, 2), (5, 2)))
    queries = draw_queries(jax.random.fold_in(jax.random.fold_in(streams_of[10], part), 71), part)
    return dict(handoff=handoff, norm_gain=norm_gain, kv_weight=kv_weight, span_start=span_start, token_owner=token_owner, token_slot=token_slot, kv_cache=kv_cache, cache_lens=cache_lens, step_kv=step_kv, queries=queries)


EPS = 1e-05
THETA = 500000.0

def rotate(pairs, positions):
    width = pairs.shape[-1] // 2
    half = width // 2
    freq = jnp.exp(-(jnp.arange(half, dtype=jnp.float32) * 2.0 / width) * math.log(THETA))
    angle = positions.astype(jnp.float32)[:, None, None] * freq[None, None, :]
    cosine = jnp.cos(angle)
    sine = jnp.sin(angle)
    first = pairs[..., :half]
    second = pairs[..., half:width]
    turned = jnp.concatenate([first * cosine - second * sine, second * cosine + first * sine], axis=-1)
    return jnp.concatenate([turned, pairs[..., width:]], axis=-1)

def attend(query, past, lens, route_pairs, route_mask, step_pairs):
    reqs, steps, heads, flat = query.shape
    width = past.shape[-1] // 2
    groups = flat // width
    scale = 1.0 / math.sqrt(width)
    qf = query.astype(jnp.float32).reshape(reqs, steps, heads, groups, width)
    pastf = past.astype(jnp.float32)
    routef = route_pairs.astype(jnp.float32)
    stepf = step_pairs.astype(jnp.float32)
    score_past = jnp.einsum('rnhgd,rphd->rnhgp', qf, pastf[..., :width]) * scale
    score_route = jnp.einsum('rnhgd,khd->rnhgk', qf, routef[..., :width]) * scale
    score_step = jnp.einsum('rnhgd,rmhd->rnhgm', qf, stepf[..., :width]) * scale
    past_mask = jnp.arange(past.shape[1], dtype=jnp.int32)[None, :] < lens[:, None]
    step_mask = jnp.arange(steps, dtype=jnp.int32)[:, None] >= jnp.arange(steps, dtype=jnp.int32)[None, :]
    score_past = jnp.where(past_mask[:, None, None, None, :], score_past, -jnp.inf)
    score_route = jnp.where(route_mask[:, None, None, None, :], score_route, -jnp.inf)
    score_step = jnp.where(step_mask[None, :, None, None, :], score_step, -jnp.inf)
    top = jnp.maximum(jnp.maximum(lax.optimization_barrier(jnp.max(score_past, axis=-1, keepdims=True)), lax.optimization_barrier(jnp.max(score_route, axis=-1, keepdims=True))), lax.optimization_barrier(jnp.max(score_step, axis=-1, keepdims=True)))
    exp_past = jnp.exp(score_past - top)
    exp_route = jnp.exp(score_route - top)
    exp_step = jnp.exp(score_step - top)
    total = lax.optimization_barrier(jnp.sum(exp_past, axis=-1, keepdims=True)) + lax.optimization_barrier(jnp.sum(exp_route, axis=-1, keepdims=True)) + lax.optimization_barrier(jnp.sum(exp_step, axis=-1, keepdims=True))
    w_past = (exp_past / total).astype(jnp.bfloat16).astype(jnp.float32)
    w_route = (exp_route / total).astype(jnp.bfloat16).astype(jnp.float32)
    w_step = (exp_step / total).astype(jnp.bfloat16).astype(jnp.float32)
    result = jnp.einsum('rnhgp,rphd->rnhgd', w_past, pastf[..., width:])
    result = result + jnp.einsum('rnhgk,khd->rnhgd', w_route, routef[..., width:])
    result = result + jnp.einsum('rnhgm,rmhd->rnhgd', w_step, stepf[..., width:])
    return result.astype(jnp.bfloat16).reshape(reqs, steps, heads, flat)

def reference(handoff, norm_gain, kv_weight, span_start, token_owner, token_slot, kv_cache, cache_lens, step_kv, queries):
    prev = jnp.roll(handoff, 1, axis=0)
    values = prev.astype(jnp.float32)
    meansq = lax.optimization_barrier(jnp.mean(values * values, axis=-1, keepdims=True))
    normed = (values * lax.rsqrt(meansq + EPS) * norm_gain[:, None, :]).astype(jnp.bfloat16)

    def project(items):
        rows, weight, start = items
        flat = weight.reshape(D, KVH * 2 * HD)
        pairs = jnp.dot(rows, flat, preferred_element_type=jnp.float32).reshape(SPAN, KVH, 2 * HD)
        positions = start + jnp.arange(SPAN, dtype=jnp.int32)
        return rotate(pairs, positions).astype(jnp.bfloat16)
    prompt_kv = lax.map(project, (normed, kv_weight, span_start))
    owners = N_SECTION * N_SEQ
    query_flat = queries.reshape(owners, LAYERS, REQ_DEV, STEPS, KVH, GQ * HD)
    cache_flat = kv_cache.reshape(owners, LAYERS, REQ_DEV, CACHE, KVH, 2 * HD)
    lens_flat = cache_lens.reshape(owners, REQ_DEV)
    step_flat = step_kv.reshape(owners, LAYERS, REQ_DEV, STEPS, KVH, 2 * HD)
    owner_ids = token_owner[..., 0]
    layered = jax.vmap(attend, in_axes=(0, 0, None, 0, 0, 0))

    def decode(items):
        index, query, past, lens, step_pairs = items
        section_id = index // N_SEQ
        shard = index % N_SEQ
        start = (shard * TOK_DEV).astype(jnp.int32)
        block = lax.dynamic_slice_in_dim(prompt_kv, start, TOK_DEV, 1)
        owned = lax.dynamic_slice_in_dim(owner_ids, start, TOK_DEV, 1)
        slots = lax.dynamic_slice_in_dim(token_slot, start, TOK_DEV, 1)
        request_ids = jnp.arange(REQ_DEV, dtype=jnp.int32)
        route_mask = (owned[:, None, :] == section_id) & (slots[:, None, :] == request_ids[None, :, None])
        return layered(query, past, lens, block, route_mask, step_pairs)
    indices = jnp.arange(owners, dtype=jnp.int32)
    outputs = lax.map(decode, (indices, query_flat, cache_flat, lens_flat, step_flat))
    return outputs.reshape(N_SECTION, N_SEQ, LAYERS, REQ_DEV, STEPS, KVH, GQ * HD)
```

```python
import math

import jax
import jax.numpy as jnp
from jax import lax
from jax.experimental import pallas as pl
from jax.experimental.pallas import tpu as pltpu
from jax.sharding import PartitionSpec as P

EPS = 1e-05
THETA = 500000.0
NEG = -1e30


def passed_along(value, axis, by):
    length = lax.axis_size(axis)
    return lax.ppermute(value, axis, [(i, (i + by) % length) for i in range(length)])


def rotate(pairs, positions):
    width = pairs.shape[-1] // 2
    half = width // 2
    freq = jnp.exp(-(jnp.arange(half, dtype=jnp.float32) * 2.0 / width) * math.log(THETA))
    angle = positions.astype(jnp.float32)[:, None, None] * freq[None, None, :]
    cosine = jnp.cos(angle)
    sine = jnp.sin(angle)
    first = pairs[..., :half]
    second = pairs[..., half:width]
    turned = jnp.concatenate(
        [first * cosine - second * sine, second * cosine + first * sine], axis=-1
    )
    return jnp.concatenate([turned, pairs[..., width:]], axis=-1)


def attend(query, past, lens, route_pairs, route_mask, step_pairs):
    reqs, steps, heads, flat = query.shape
    width = past.shape[-1] // 2
    groups = flat // width
    scale = 1.0 / math.sqrt(width)
    shaped = query.reshape(reqs, steps, heads, groups, width)
    score_past = (
        jnp.einsum(
            "rnhgd,rphd->rnhgp", shaped, past[..., :width], preferred_element_type=jnp.float32
        )
        * scale
    )
    score_route = (
        jnp.einsum(
            "rnhgd,khd->rnhgk", shaped, route_pairs[..., :width], preferred_element_type=jnp.float32
        )
        * scale
    )
    score_step = (
        jnp.einsum(
            "rnhgd,rmhd->rnhgm", shaped, step_pairs[..., :width], preferred_element_type=jnp.float32
        )
        * scale
    )
    past_mask = jnp.arange(past.shape[1], dtype=jnp.int32)[None, :] < lens[:, None]
    step_mask = (
        jnp.arange(steps, dtype=jnp.int32)[:, None] >= jnp.arange(steps, dtype=jnp.int32)[None, :]
    )
    score_past = jnp.where(past_mask[:, None, None, None, :], score_past, -jnp.inf)
    score_route = jnp.where(route_mask[:, None, None, None, :], score_route, -jnp.inf)
    score_step = jnp.where(step_mask[None, :, None, None, :], score_step, -jnp.inf)
    top = jnp.maximum(
        jnp.maximum(
            jnp.max(score_past, axis=-1, keepdims=True),
            jnp.max(score_route, axis=-1, keepdims=True),
        ),
        jnp.max(score_step, axis=-1, keepdims=True),
    )
    exp_past = jnp.exp(score_past - top)
    exp_route = jnp.exp(score_route - top)
    exp_step = jnp.exp(score_step - top)
    total = (
        jnp.sum(exp_past, axis=-1, keepdims=True)
        + jnp.sum(exp_route, axis=-1, keepdims=True)
        + jnp.sum(exp_step, axis=-1, keepdims=True)
    )
    w_past = (exp_past / total).astype(jnp.bfloat16)
    w_route = (exp_route / total).astype(jnp.bfloat16)
    w_step = (exp_step / total).astype(jnp.bfloat16)
    result = jnp.einsum(
        "rnhgp,rphd->rnhgd", w_past, past[..., width:], preferred_element_type=jnp.float32
    )
    result = result + jnp.einsum(
        "rnhgk,khd->rnhgd", w_route, route_pairs[..., width:], preferred_element_type=jnp.float32
    )
    result = result + jnp.einsum(
        "rnhgm,rmhd->rnhgd", w_step, step_pairs[..., width:], preferred_element_type=jnp.float32
    )
    return result.astype(jnp.bfloat16).reshape(reqs, steps, heads, flat)


def local(
    handoff,
    norm_gain,
    kv_weight,
    span_start,
    token_owner,
    token_slot,
    kv_cache,
    cache_lens,
    step_kv,
    queries,
):
    received = passed_along(handoff, "section", 1)
    whole = lax.all_gather(received[0], "tp", axis=1, tiled=True)
    tokens = whole.shape[0]
    values = whole.astype(jnp.float32)
    meansq = jnp.mean(values * values, axis=-1, keepdims=True)
    normed = (values * lax.rsqrt(meansq + EPS) * norm_gain[0][None, :]).astype(jnp.bfloat16)
    weight = kv_weight[0]
    local_heads = weight.shape[1]
    pair_width = weight.shape[2]
    columns_out = local_heads * pair_width
    piece = lax.all_gather(weight, "seq", axis=0, tiled=True)
    projected = jnp.dot(
        normed, piece.reshape(piece.shape[0], columns_out), preferred_element_type=jnp.float32
    )
    positions = span_start[0] + lax.axis_index("seq") * tokens + jnp.arange(tokens, dtype=jnp.int32)
    prompt_kv = rotate(projected.reshape(tokens, local_heads, pair_width), positions).astype(
        jnp.bfloat16
    )
    sections = lax.axis_size("section")
    capacity = 2 * tokens // sections
    owner = token_owner[0, :, 0]
    slot = token_slot[0]
    onehot = (owner[:, None] == jnp.arange(sections, dtype=jnp.int32)[None, :]).astype(jnp.bfloat16)
    lower = (
        jnp.arange(tokens, dtype=jnp.int32)[:, None] >= jnp.arange(tokens, dtype=jnp.int32)[None, :]
    ).astype(jnp.bfloat16)
    running = jnp.dot(lower, onehot, preferred_element_type=jnp.float32)
    rank = (jnp.sum(running * onehot.astype(jnp.float32), axis=1) - 1.0).astype(jnp.int32)
    place = owner * capacity + rank
    select = (place[:, None] == jnp.arange(sections * capacity, dtype=jnp.int32)[None, :]).astype(
        jnp.bfloat16
    )
    packed = jnp.einsum(
        "ts,tc->sc",
        select,
        prompt_kv.reshape(tokens, columns_out),
        preferred_element_type=jnp.float32,
    )
    packed = packed.astype(jnp.bfloat16).reshape(sections, capacity, local_heads, pair_width)
    labels = jnp.einsum(
        "ts,t->s", select, (slot + 1).astype(jnp.bfloat16), preferred_element_type=jnp.float32
    )
    labels = labels.astype(jnp.bfloat16).reshape(sections, capacity)
    routed, routed_labels = (
        lax.all_to_all(packed, "section", split_axis=0, concat_axis=0, tiled=True),
        lax.all_to_all(labels, "section", split_axis=0, concat_axis=0, tiled=True),
    )
    request_ids = (jnp.arange(kv_cache.shape[3], dtype=jnp.int32) + 1).astype(jnp.float32)
    route_mask = routed_labels.astype(jnp.float32)[:, None, :] == request_ids[None, :, None]
    layered = jax.vmap(attend, in_axes=(0, 0, None, 0, 0, 0))
    result = layered(
        queries[0, 0], kv_cache[0, 0], cache_lens[0, 0], routed, route_mask, step_kv[0, 0]
    )
    return result[None, None]


def steered(value, pairs_of, sizes):
    groups, seqs, cores = sizes
    pairs = []
    for g in range(groups):
        for q in range(seqs):
            for t in range(cores):
                a, b, c = pairs_of(g, q, t)
                pairs.append(((g * seqs + q) * cores + t, (a * seqs + b) * cores + c))
    return lax.ppermute(value, ("group", "seq", "tp"), pairs)


def swapped(value):
    return lax.ppermute(value, "tp", [(0, 1), (1, 0)])


def split_heads(mixed, gain, joined, blocks):
    rows = mixed.shape[0] // 2
    width = mixed.shape[1]
    tall = rows // blocks

    def body(mixed_ref, gain_ref, *rest):
        outs, wide = rest[:-1], rest[-1]
        wide[...] = mixed_ref[...].astype(jnp.float32)
        gains = jnp.concatenate(
            [
                jnp.broadcast_to(gain_ref[:, b * width : (b + 1) * width], (width, width)).T
                for b in range(tall // width)
            ],
            axis=0,
        )
        for head in range(2):
            scaled = (wide[pl.ds(head, tall, stride=2), :] * gains).astype(jnp.bfloat16)
            if joined:
                outs[0][:, head * width : (head + 1) * width] = scaled
            else:
                outs[head][...] = scaled

    if joined:
        shapes = [jax.ShapeDtypeStruct((rows, 2 * width), jnp.bfloat16)]
        out_specs = [pl.BlockSpec((tall, 2 * width), lambda i: (i, 0))]
    else:
        shapes = [jax.ShapeDtypeStruct((rows, width), jnp.bfloat16)] * 2
        out_specs = [pl.BlockSpec((tall, width), lambda i: (i, 0))] * 2
    return pl.pallas_call(
        body,
        out_shape=shapes,
        grid=(blocks,),
        in_specs=[
            pl.BlockSpec((2 * tall, width), lambda i: (i, 0)),
            pl.BlockSpec((1, tall), lambda i: (0, i)),
        ],
        out_specs=out_specs,
        scratch_shapes=[pltpu.VMEM((2 * tall, width), jnp.float32)],
        name="split_heads",
    )(mixed, gain)


def partial_products(same, acts, weights):
    tokens = acts[0].shape[0]
    columns = weights[0].shape[1]
    depths = [w.shape[0] for w in weights]

    def body(same_ref, near_ref, near_mate_ref, far_ref, far_mate_ref, *rest):
        w_refs, outs = rest[: len(depths)], rest[len(depths) :]

        def product(ref):
            total = None
            start = 0
            for w_ref, depth in zip(w_refs, depths):
                part = jnp.dot(
                    ref[:, start : start + depth], w_ref[...], preferred_element_type=jnp.float32
                )
                total = part if total is None else total + part
                start += depth
            return total

        def fill(own, across, far_own, far_across):
            outs[1][...] = product(across).astype(jnp.bfloat16)
            outs[2][...] = product(far_own).astype(jnp.bfloat16)
            outs[3][...] = product(far_across).astype(jnp.bfloat16)
            outs[0][...] = product(own)

        @pl.when(same_ref[0] == 1)
        def _():
            fill(near_ref, near_mate_ref, far_ref, far_mate_ref)

        @pl.when(same_ref[0] == 0)
        def _():
            fill(near_mate_ref, near_ref, far_mate_ref, far_ref)

    vmem = pl.BlockSpec(memory_space=pltpu.VMEM)
    return pl.pallas_call(
        body,
        out_shape=[jax.ShapeDtypeStruct((tokens, columns), jnp.float32)]
        + [jax.ShapeDtypeStruct((tokens, columns), jnp.bfloat16)] * 3,
        in_specs=[pl.BlockSpec(memory_space=pltpu.SMEM)] + [vmem] * (4 + len(weights)),
        out_specs=[vmem] * 4,
        compiler_params=pltpu.CompilerParams(vmem_limit_bytes=40 << 20),
        name="partial_products",
    )(same, *acts, *weights)


def summed_over_chips(parts, sizes):
    own, across, far, far_across = parts
    groups, seqs, _ = sizes
    return (
        own,
        steered(across, lambda g, q, t: (g, seqs - 1 - q, t), sizes),
        steered(far, lambda g, q, t: (groups - 1 - g, q, t), sizes),
        steered(far_across, lambda g, q, t: (groups - 1 - g, seqs - 1 - q, t), sizes),
    )


def attend_routed(asked, keys, values, scale, cosine, sine, code):
    owners, heads, rows, width = asked.shape
    tokens = code.shape[1]
    half = width // 2
    requests = 2
    factor = 1.0 / math.sqrt(width)

    def body(asked_ref, *rest):
        key_refs = rest[:4]
        value_refs = [rest[4 + 4 * h : 8 + 4 * h] for h in range(heads)]
        scale_ref, cos_ref, sin_ref, code_ref, out_ref = rest[4 + 4 * heads :]
        span = owners * rows
        request = lax.broadcasted_iota(jnp.int32, (span, tokens), 0) // (rows // requests)
        mine = request == code_ref[...]
        lane = lax.broadcasted_iota(jnp.int32, (span, width), 1)
        for h in range(heads):
            columns = slice(h * width, (h + 1) * width)
            key = key_refs[0][:, columns]
            for ref in key_refs[1:]:
                key = key + ref[:, columns].astype(jnp.float32)
            key = key * scale_ref[...]
            first = key[:, :half]
            second = key[:, half:]
            cosine_ = cos_ref[...]
            sine_ = sin_ref[...]
            key = jnp.concatenate(
                [first * cosine_ - second * sine_, second * cosine_ + first * sine_], axis=1
            ).astype(jnp.bfloat16)
            value = value_refs[h][0][...]
            for ref in value_refs[h][1:]:
                value = value + ref[...].astype(jnp.float32)
            value = (value * scale_ref[...]).astype(jnp.bfloat16)
            query = jnp.concatenate([asked_ref[o, h] for o in range(owners)], axis=0)
            score = (
                lax.dot_general(
                    query, key, (((1,), (1,)), ((), ())), preferred_element_type=jnp.float32
                )
                * factor
            )
            score = jnp.where(mine, score, NEG)
            top = jnp.max(score, axis=1, keepdims=True)
            weight = jnp.where(mine, jnp.exp(score - top), 0.0)
            total = jnp.sum(weight, axis=1, keepdims=True)
            mixed = jnp.dot(
                weight.astype(jnp.bfloat16), value, preferred_element_type=jnp.float32
            )
            some = total > 0.0
            safe = jnp.where(some, total, 1.0)
            mixed = (mixed / safe).astype(jnp.bfloat16)
            level = jnp.where(some, top + jnp.log(safe), NEG)
            high = level.astype(jnp.bfloat16).astype(jnp.float32)
            middle = (level - high).astype(jnp.bfloat16).astype(jnp.float32)
            low = level - high - middle
            marks = jnp.where(
                lane == 0, high, jnp.where(lane == 1, middle, jnp.where(lane == 2, low, 0.0))
            ).astype(jnp.bfloat16)
            for o in range(owners):
                out_ref[o, h, :, :width] = mixed[o * rows : (o + 1) * rows]
                out_ref[o, h, :, width:] = marks[o * rows : (o + 1) * rows]

    vmem = pl.BlockSpec(memory_space=pltpu.VMEM)
    operands = (asked, *keys, *[v for chunk in values for v in chunk], scale, cosine, sine, code)
    return pl.pallas_call(
        body,
        out_shape=jax.ShapeDtypeStruct((owners, heads, rows, 2 * width), jnp.bfloat16),
        in_specs=[vmem] * len(operands),
        out_specs=vmem,
        name="attend_routed",
    )(*operands)


def attend_kept(query, past, lens, step_pairs):
    layers, reqs, steps, heads, flat = query.shape
    width = past.shape[-1] // 2
    scale = 1.0 / math.sqrt(width)
    shaped = query.reshape(layers, reqs, steps, heads, flat // width, width)
    score_past = scale * jnp.einsum(
        "lrnhgd,lrphd->lrhngp", shaped, past[..., :width], preferred_element_type=jnp.float32
    )
    score_step = scale * jnp.einsum(
        "lrnhgd,lrmhd->lrhngm", shaped, step_pairs[..., :width], preferred_element_type=jnp.float32
    )
    filled = jnp.arange(past.shape[2], dtype=jnp.int32)[None, :] < lens[:, None]
    turn = jnp.arange(steps, dtype=jnp.int32)
    score_past = jnp.where(filled[None, :, None, None, None, :], score_past, NEG)
    score_step = jnp.where(
        (turn[:, None] >= turn[None, :])[None, None, None, :, None, :], score_step, NEG
    )
    top = jnp.maximum(
        jnp.max(score_past, axis=-1, keepdims=True), jnp.max(score_step, axis=-1, keepdims=True)
    )
    exp_past = jnp.exp(score_past - top)
    exp_step = jnp.exp(score_step - top)
    total = jnp.sum(exp_past, axis=-1, keepdims=True) + jnp.sum(exp_step, axis=-1, keepdims=True)
    mixed = jnp.einsum(
        "lrhngp,lrphd->lrhngd",
        exp_past.astype(jnp.bfloat16),
        past[..., width:],
        preferred_element_type=jnp.float32,
    ) + jnp.einsum(
        "lrhngm,lrmhd->lrhngd",
        exp_step.astype(jnp.bfloat16),
        step_pairs[..., width:],
        preferred_element_type=jnp.float32,
    )
    return mixed, top, total


def meet_local(
    handoff,
    norm_gain,
    kv_weight,
    span_start,
    token_owner,
    token_slot,
    kv_cache,
    cache_lens,
    step_kv,
    queries,
):
    sizes = (lax.axis_size("group"), lax.axis_size("seq"), lax.axis_size("tp"))
    sections = lax.axis_size("section")
    g = lax.axis_index("group")
    q = lax.axis_index("seq")
    t = lax.axis_index("tp")
    weight = kv_weight[0]
    depth = weight.shape[0] // sizes[0]
    width = weight.shape[2] // 2
    first = depth // 4

    gain = lax.dynamic_slice_in_dim(norm_gain[0], (q * sizes[0] + g) * depth, depth, 0)[None]

    def piece(start, rows, column):
        cut = lax.dynamic_slice(weight, (g * depth + start, 0, column * width), (rows, 2, width))
        return cut.reshape(2 * rows, width)

    (keys_a,) = split_heads(piece(0, first, 0), gain[:, :first], True, 1)
    (keys_b,) = split_heads(piece(first, depth - first, 0), gain[:, first:], True, 3)
    values_0, values_1 = split_heads(piece(0, depth, 1), gain, False, 4)
    keys_a = passed_along(keys_a, "section", -1)
    keys_b = passed_along(keys_b, "section", -1)
    values_0 = passed_along(values_0, "section", -1)
    values_1 = passed_along(values_1, "section", -1)

    block = handoff[0]
    tokens = block.shape[0]
    near = lax.dynamic_slice_in_dim(block, g * depth, depth, 1)
    far = lax.dynamic_slice_in_dim(block, (sizes[0] - 1 - g) * depth, depth, 1)
    near = steered(near, lambda a, b, c: (a, c, b), sizes)
    far = steered(far, lambda a, b, c: (sizes[0] - 1 - a, c, b), sizes)
    acts = (near, swapped(near), far, swapped(far))
    same = (q == t).astype(jnp.int32)[None]

    wide = block.astype(jnp.float32)
    square = jnp.sum(wide * wide, axis=-1, keepdims=True)
    square = square + swapped(square)
    scale = lax.rsqrt(square / (block.shape[1] * sizes[2]) + EPS)

    code = token_owner[0, :, 0] * 2 + token_slot[0]
    notes = jnp.concatenate([code, jnp.broadcast_to(span_start, (width,))])[None]
    notes = passed_along(notes, "section", -1)
    code = notes[:, :tokens]
    positions = notes[0, tokens] + q * tokens + jnp.arange(tokens, dtype=jnp.int32)
    half = width // 2
    freq = jnp.exp(-(jnp.arange(half, dtype=jnp.float32) * 2.0 / width) * math.log(THETA))
    angle = positions.astype(jnp.float32)[:, None] * freq[None, :]
    cosine = jnp.cos(angle)
    sine = jnp.sin(angle)

    query = queries[0, 0]
    layers, reqs, steps, heads, flat = query.shape
    rows = reqs * steps * flat // width
    asked = query.reshape(layers, reqs, steps, heads, flat // width, width)
    asked = asked.transpose(0, 3, 1, 2, 4, 5).reshape(layers, heads, rows, width)
    asked = lax.all_to_all(
        jnp.roll(asked, -1, axis=0), "section", split_axis=0, concat_axis=0, tiled=True
    )

    keys = summed_over_chips(partial_products(same, acts, (keys_a, keys_b)), sizes)
    values = [
        summed_over_chips(partial_products(same, acts, (v,)), sizes) for v in (values_0, values_1)
    ]
    routed = attend_routed(asked, keys, values, scale, cosine, sine, code)
    routed = lax.all_to_all(routed, "section", split_axis=0, concat_axis=0, tiled=True)
    routed = jnp.roll(routed, 1, axis=0)
    routed = routed.reshape(layers, heads, reqs, steps, flat // width, 2 * width)
    routed = routed.transpose(0, 2, 1, 3, 4, 5).astype(jnp.float32)
    level = jnp.sum(routed[..., width : width + 3], axis=-1, keepdims=True)
    mixed, top, total = attend_kept(query, kv_cache[0, 0], cache_lens[0, 0], step_kv[0, 0])
    peak = jnp.maximum(level, top)
    kept_part = jnp.exp(top - peak)
    routed_part = jnp.exp(level - peak)
    result = (mixed * kept_part + routed[..., :width] * routed_part) / (
        total * kept_part + routed_part
    )
    result = result.astype(jnp.bfloat16).transpose(0, 1, 3, 2, 4, 5)
    return result.reshape(layers, reqs, steps, heads, flat)[None, None]


def solution(mesh):
    shape = mesh.shape
    body = meet_local if shape["group"] == shape["seq"] == shape["tp"] == 2 else local
    return jax.shard_map(
        body,
        mesh=mesh,
        in_specs=(
            P(("group", "section"), "seq", "tp"),
            P("section", None),
            P("section", "seq", "tp", None),
            P(("group", "section")),
            P(("group", "section"), "seq", None),
            P(("group", "section"), "seq"),
            P(("group", "section"), "seq", None, None, None, "tp", None),
            P(("group", "section"), "seq", None),
            P(("group", "section"), "seq", None, None, None, "tp", None),
            P(("group", "section"), "seq", None, None, None, "tp", None),
        ),
        out_specs=P(("group", "section"), "seq", None, None, None, "tp", None),
        check_vma=False,
    )
```

```python
import math

import jax
import jax.numpy as jnp
from jax import lax
from jax.experimental import pallas as pl
from jax.experimental.pallas import tpu as pltpu
from jax.sharding import PartitionSpec as P

EPS = 1e-05
THETA = 500000.0
NEG = -1e30


def passed_along(value, axis, by):
    length = lax.axis_size(axis)
    return lax.ppermute(value, axis, [(i, (i + by) % length) for i in range(length)])


def rotate(pairs, positions):
    width = pairs.shape[-1] // 2
    half = width // 2
    freq = jnp.exp(-(jnp.arange(half, dtype=jnp.float32) * 2.0 / width) * math.log(THETA))
    angle = positions.astype(jnp.float32)[:, None, None] * freq[None, None, :]
    cosine = jnp.cos(angle)
    sine = jnp.sin(angle)
    first = pairs[..., :half]
    second = pairs[..., half:width]
    turned = jnp.concatenate(
        [first * cosine - second * sine, second * cosine + first * sine], axis=-1
    )
    return jnp.concatenate([turned, pairs[..., width:]], axis=-1)


def attend(query, past, lens, route_pairs, route_mask, step_pairs):
    reqs, steps, heads, flat = query.shape
    width = past.shape[-1] // 2
    groups = flat // width
    scale = 1.0 / math.sqrt(width)
    shaped = query.reshape(reqs, steps, heads, groups, width)
    score_past = (
        jnp.einsum(
            "rnhgd,rphd->rnhgp", shaped, past[..., :width], preferred_element_type=jnp.float32
        )
        * scale
    )
    score_route = (
        jnp.einsum(
            "rnhgd,khd->rnhgk", shaped, route_pairs[..., :width], preferred_element_type=jnp.float32
        )
        * scale
    )
    score_step = (
        jnp.einsum(
            "rnhgd,rmhd->rnhgm", shaped, step_pairs[..., :width], preferred_element_type=jnp.float32
        )
        * scale
    )
    past_mask = jnp.arange(past.shape[1], dtype=jnp.int32)[None, :] < lens[:, None]
    step_mask = (
        jnp.arange(steps, dtype=jnp.int32)[:, None] >= jnp.arange(steps, dtype=jnp.int32)[None, :]
    )
    score_past = jnp.where(past_mask[:, None, None, None, :], score_past, -jnp.inf)
    score_route = jnp.where(route_mask[:, None, None, None, :], score_route, -jnp.inf)
    score_step = jnp.where(step_mask[None, :, None, None, :], score_step, -jnp.inf)
    top = jnp.maximum(
        jnp.maximum(
            jnp.max(score_past, axis=-1, keepdims=True),
            jnp.max(score_route, axis=-1, keepdims=True),
        ),
        jnp.max(score_step, axis=-1, keepdims=True),
    )
    exp_past = jnp.exp(score_past - top)
    exp_route = jnp.exp(score_route - top)
    exp_step = jnp.exp(score_step - top)
    total = (
        jnp.sum(exp_past, axis=-1, keepdims=True)
        + jnp.sum(exp_route, axis=-1, keepdims=True)
        + jnp.sum(exp_step, axis=-1, keepdims=True)
    )
    w_past = (exp_past / total).astype(jnp.bfloat16)
    w_route = (exp_route / total).astype(jnp.bfloat16)
    w_step = (exp_step / total).astype(jnp.bfloat16)
    result = jnp.einsum(
        "rnhgp,rphd->rnhgd", w_past, past[..., width:], preferred_element_type=jnp.float32
    )
    result = result + jnp.einsum(
        "rnhgk,khd->rnhgd", w_route, route_pairs[..., width:], preferred_element_type=jnp.float32
    )
    result = result + jnp.einsum(
        "rnhgm,rmhd->rnhgd", w_step, step_pairs[..., width:], preferred_element_type=jnp.float32
    )
    return result.astype(jnp.bfloat16).reshape(reqs, steps, heads, flat)


def local(
    handoff,
    norm_gain,
    kv_weight,
    span_start,
    token_owner,
    token_slot,
    kv_cache,
    cache_lens,
    step_kv,
    queries,
):
    received = passed_along(handoff, "section", 1)
    whole = lax.all_gather(received[0], "tp", axis=1, tiled=True)
    tokens = whole.shape[0]
    values = whole.astype(jnp.float32)
    meansq = jnp.mean(values * values, axis=-1, keepdims=True)
    normed = (values * lax.rsqrt(meansq + EPS) * norm_gain[0][None, :]).astype(jnp.bfloat16)
    weight = kv_weight[0]
    local_heads = weight.shape[1]
    pair_width = weight.shape[2]
    columns_out = local_heads * pair_width
    piece = lax.all_gather(weight, "seq", axis=0, tiled=True)
    projected = jnp.dot(
        normed, piece.reshape(piece.shape[0], columns_out), preferred_element_type=jnp.float32
    )
    positions = span_start[0] + lax.axis_index("seq") * tokens + jnp.arange(tokens, dtype=jnp.int32)
    prompt_kv = rotate(projected.reshape(tokens, local_heads, pair_width), positions).astype(
        jnp.bfloat16
    )
    sections = lax.axis_size("section")
    capacity = 2 * tokens // sections
    owner = token_owner[0, :, 0]
    slot = token_slot[0]
    onehot = (owner[:, None] == jnp.arange(sections, dtype=jnp.int32)[None, :]).astype(jnp.bfloat16)
    lower = (
        jnp.arange(tokens, dtype=jnp.int32)[:, None] >= jnp.arange(tokens, dtype=jnp.int32)[None, :]
    ).astype(jnp.bfloat16)
    running = jnp.dot(lower, onehot, preferred_element_type=jnp.float32)
    rank = (jnp.sum(running * onehot.astype(jnp.float32), axis=1) - 1.0).astype(jnp.int32)
    place = owner * capacity + rank
    select = (place[:, None] == jnp.arange(sections * capacity, dtype=jnp.int32)[None, :]).astype(
        jnp.bfloat16
    )
    packed = jnp.einsum(
        "ts,tc->sc",
        select,
        prompt_kv.reshape(tokens, columns_out),
        preferred_element_type=jnp.float32,
    )
    packed = packed.astype(jnp.bfloat16).reshape(sections, capacity, local_heads, pair_width)
    labels = jnp.einsum(
        "ts,t->s", select, (slot + 1).astype(jnp.bfloat16), preferred_element_type=jnp.float32
    )
    labels = labels.astype(jnp.bfloat16).reshape(sections, capacity)
    routed, routed_labels = (
        lax.all_to_all(packed, "section", split_axis=0, concat_axis=0, tiled=True),
        lax.all_to_all(labels, "section", split_axis=0, concat_axis=0, tiled=True),
    )
    request_ids = (jnp.arange(kv_cache.shape[3], dtype=jnp.int32) + 1).astype(jnp.float32)
    route_mask = routed_labels.astype(jnp.float32)[:, None, :] == request_ids[None, :, None]
    layered = jax.vmap(attend, in_axes=(0, 0, None, 0, 0, 0))
    result = layered(
        queries[0, 0], kv_cache[0, 0], cache_lens[0, 0], routed, route_mask, step_kv[0, 0]
    )
    return result[None, None]


def steered(value, pairs_of, sizes):
    groups, seqs, cores = sizes
    pairs = []
    for g in range(groups):
        for q in range(seqs):
            for t in range(cores):
                a, b, c = pairs_of(g, q, t)
                pairs.append(((g * seqs + q) * cores + t, (a * seqs + b) * cores + c))
    return lax.ppermute(value, ("group", "seq", "tp"), pairs)


def swapped(value):
    return lax.ppermute(value, "tp", [(0, 1), (1, 0)])


def after(value, early):
    return lax.optimization_barrier((value, early))[0]


def split_heads(rows4, gain, group, quarter, depth, start, count, blocks, parts, notes=None):
    width = rows4.shape[1]
    tall = count // blocks
    columns = 4 * width // parts
    extra = 0 if notes is None else 16

    def body(group_ref, quarter_ref, mixed_ref, gain_ref, *rest):
        outs, wide = rest[len(rest) - 1 - parts : -1], rest[-1]
        wide[...] = mixed_ref[...].astype(jnp.float32)
        gains = jnp.concatenate(
            [
                jnp.broadcast_to(gain_ref[:, b * width : (b + 1) * width], (width, width)).T
                for b in range(tall // width)
            ],
            axis=0,
        )
        for kind in range(2):
            for head in range(2):
                scaled = wide[pl.ds(2 * kind + head, tall, stride=4), :] * gains
                column = (2 * kind + head) * width
                out = outs[column * parts // (4 * width)]
                column = column % (4 * width // parts)
                out[:tall, column : column + width] = scaled.astype(jnp.bfloat16)
        if extra:
            outs[0][tall:, :] = jnp.broadcast_to(rest[0][...], (extra, columns)).astype(jnp.bfloat16)

    operands = [group, quarter, rows4, gain]
    in_specs = [
        pl.BlockSpec(
            (4 * tall, width),
            lambda i, group, quarter: (group[0] * (depth // tall) + start // tall + i, 0),
        ),
        pl.BlockSpec(
            (1, tall),
            lambda i, group, quarter: (0, quarter[0] * (depth // tall) + start // tall + i),
        ),
    ]
    if extra:
        operands.append(notes)
        in_specs.append(pl.BlockSpec((1, columns), lambda i, group, quarter: (0, 0)))
    return pl.pallas_call(
        body,
        out_shape=[jax.ShapeDtypeStruct((count + extra, columns), jnp.bfloat16)] * parts,
        grid_spec=pltpu.PrefetchScalarGridSpec(
            num_scalar_prefetch=2,
            grid=(blocks,),
            in_specs=in_specs,
            out_specs=[pl.BlockSpec((tall + extra, columns), lambda i, group, quarter: (i, 0))]
            * parts,
            scratch_shapes=[pltpu.VMEM((4 * tall, width), jnp.float32)],
        ),
        compiler_params=pltpu.CompilerParams(vmem_limit_bytes=60 << 20),
        name="split_heads",
    )(*operands)


def cut_columns(block, group, depth, cuts):
    tokens = block.shape[0]

    def body(group_ref, block_ref, *rest):
        outs, sems = rest[:-1], rest[-1]
        copies = []
        for n, (other, start, count) in enumerate(cuts):
            which = (1 - group_ref[0]) if other else group_ref[0]
            column = pl.multiple_of(which * depth + start, 128)
            copies.append(
                pltpu.make_async_copy(block_ref.at[:, pl.ds(column, count)], outs[n], sems.at[n])
            )
        for copy in copies:
            copy.start()
        for copy in copies:
            copy.wait()

    anywhere = pl.BlockSpec(memory_space=pl.ANY)
    return pl.pallas_call(
        body,
        out_shape=[jax.ShapeDtypeStruct((tokens, count), block.dtype) for _, _, count in cuts],
        in_specs=[pl.BlockSpec(memory_space=pltpu.SMEM), anywhere],
        out_specs=[pl.BlockSpec(memory_space=pltpu.VMEM)] * len(cuts),
        scratch_shapes=[pltpu.SemaphoreType.DMA((len(cuts),))],
        compiler_params=pltpu.CompilerParams(vmem_limit_bytes=60 << 20),
        name="cut_columns",
    )(group, block)


def partial_products(same, pairs, weights, first_column, columns, first_kind):
    tokens = pairs[0][0][0].shape[0]
    depth = pairs[0][0][0].shape[1]
    acts = [piece for pair in pairs for side in pair for piece in side]
    count = len(acts) + len(weights)

    def body(same_ref, *refs):
        act_refs = refs[: len(acts)]
        weight_refs = refs[len(acts) : count]
        outs = refs[count : count + 2 * len(pairs)]
        held, weight, sems = refs[count + 2 * len(pairs) :]
        weight_copies = []
        row = 0
        for n, ref in enumerate(weight_refs):
            taken = min(ref.shape[0], depth - row) // 128 * 128
            column = first_column if ref.shape[1] > columns else 0
            weight_copies.append(
                pltpu.make_async_copy(
                    ref.at[pl.ds(0, taken), pl.ds(column, columns)],
                    weight.at[pl.ds(row, taken), :],
                    sems.at[len(acts) + n],
                )
            )
            row += taken
        for copy in weight_copies:
            copy.start()
        act_copies = []
        n = 0
        for p, pair in enumerate(pairs):
            mine = []
            for side in range(2):
                slot = 2 * p + ((1 - same_ref[0]) if side == 0 else same_ref[0])
                column = 0
                for piece in pair[side]:
                    wide = piece.shape[1]
                    copy = pltpu.make_async_copy(
                        act_refs[n], held.at[slot, :, pl.ds(column, wide)], sems.at[n]
                    )
                    copy.start()
                    mine.append(copy)
                    column += wide
                    n += 1
            act_copies.append(mine)
        for copy in weight_copies:
            copy.wait()
        for p in range(len(pairs)):
            for copy in act_copies[p]:
                copy.wait()
            for side in range(2):
                out = outs[2 * p + side]
                out[...] = jnp.dot(
                    held[2 * p + side], weight[...], preferred_element_type=jnp.float32
                ).astype(out.dtype)

    anywhere = pl.BlockSpec(memory_space=pl.ANY)
    vmem = pl.BlockSpec(memory_space=pltpu.VMEM)
    kinds = [jnp.float32, jnp.bfloat16, jnp.bfloat16, jnp.bfloat16]
    kinds = kinds[first_kind : first_kind + 2 * len(pairs)]
    return pl.pallas_call(
        body,
        out_shape=[jax.ShapeDtypeStruct((tokens, columns), kind) for kind in kinds],
        in_specs=[pl.BlockSpec(memory_space=pltpu.SMEM)] + [anywhere] * count,
        out_specs=[vmem] * len(kinds),
        scratch_shapes=[
            pltpu.VMEM((2 * len(pairs), tokens, depth), jnp.bfloat16),
            pltpu.VMEM((depth, columns), jnp.bfloat16),
            pltpu.SemaphoreType.DMA((count,)),
        ],
        compiler_params=pltpu.CompilerParams(vmem_limit_bytes=(5 + 4 * len(pairs)) << 20),
        name="partial_products",
    )(same, *acts, *weights)


def summed_over_chips(parts, sizes):
    own, across, far, far_across = parts
    groups, seqs, _ = sizes
    return (
        own,
        steered(across, lambda g, q, t: (g, seqs - 1 - q, t), sizes),
        steered(far, lambda g, q, t: (groups - 1 - g, q, t), sizes),
        steered(far_across, lambda g, q, t: (groups - 1 - g, seqs - 1 - q, t), sizes),
    )


def weigh(asked, keys, square, cosine, sine, code, features):
    owners, heads, rows, width = asked.shape
    tokens = code.shape[1]
    half = width // 2
    requests = 2
    factor = 1.0 / math.sqrt(width)
    span = owners * rows

    def body(asked_ref, *rest):
        key_refs = rest[:4]
        square_ref, cos_ref, sin_ref, code_ref, weight_ref, mark_ref = rest[4:]
        scale = lax.rsqrt(square_ref[...] / features + EPS)
        request = lax.broadcasted_iota(jnp.int32, (span, tokens), 0) // (rows // requests)
        mine = request == code_ref[...]
        lane = lax.broadcasted_iota(jnp.int32, (span, width), 1)
        for h in range(heads):
            columns = slice(h * width, (h + 1) * width)
            key = key_refs[0][:, columns]
            for ref in key_refs[1:]:
                key = key + ref[:, columns].astype(jnp.float32)
            first = key[:, :half]
            second = key[:, half:]
            key = jnp.concatenate(
                [
                    first * cos_ref[...] - second * sin_ref[...],
                    second * cos_ref[...] + first * sin_ref[...],
                ],
                axis=1,
            ).astype(jnp.bfloat16)
            query = jnp.concatenate([asked_ref[o, h] for o in range(owners)], axis=0)
            score = lax.dot_general(
                query, key, (((1,), (1,)), ((), ())), preferred_element_type=jnp.float32
            ) * (scale * factor)
            score = jnp.where(mine, score, NEG)
            top = jnp.max(score, axis=1, keepdims=True)
            weight = jnp.where(mine, jnp.exp(score - top), 0.0)
            total = jnp.sum(weight, axis=1, keepdims=True)
            some = total > 0.0
            safe = jnp.where(some, total, 1.0)
            weight_ref[h] = (weight / safe * scale).astype(jnp.bfloat16)
            level = jnp.where(some, top + jnp.log(safe), NEG)
            high = level.astype(jnp.bfloat16).astype(jnp.float32)
            middle = (level - high).astype(jnp.bfloat16).astype(jnp.float32)
            low = level - high - middle
            mark_ref[h] = jnp.where(
                lane == 0, high, jnp.where(lane == 1, middle, jnp.where(lane == 2, low, 0.0))
            ).astype(jnp.bfloat16)

    vmem = pl.BlockSpec(memory_space=pltpu.VMEM)
    operands = (asked, *keys, square, cosine, sine, code)
    return pl.pallas_call(
        body,
        out_shape=[
            jax.ShapeDtypeStruct((heads, span, tokens), jnp.bfloat16),
            jax.ShapeDtypeStruct((heads, span, width), jnp.bfloat16),
        ],
        in_specs=[vmem] * len(operands),
        out_specs=[vmem] * 2,
        compiler_params=pltpu.CompilerParams(vmem_limit_bytes=6 << 20),
        name="weigh",
    )(*operands)


def mix(weights, marks, values, owners):
    heads, span, _ = weights.shape
    width = marks.shape[2]
    rows = span // owners

    def body(weight_ref, mark_ref, *rest):
        value_refs, out_ref = rest[:-1], rest[-1]
        for h in range(heads):
            columns = slice(h * width, (h + 1) * width)
            value = value_refs[0][:, columns]
            for ref in value_refs[1:]:
                value = value + ref[:, columns].astype(jnp.float32)
            mixed = jnp.dot(
                weight_ref[h], value.astype(jnp.bfloat16), preferred_element_type=jnp.float32
            ).astype(jnp.bfloat16)
            for o in range(owners):
                out_ref[o, h, :, :width] = mixed[o * rows : (o + 1) * rows]
                out_ref[o, h, :, width:] = mark_ref[h, o * rows : (o + 1) * rows, :]

    vmem = pl.BlockSpec(memory_space=pltpu.VMEM)
    operands = (weights, marks, *values)
    return pl.pallas_call(
        body,
        out_shape=jax.ShapeDtypeStruct((owners, heads, rows, 2 * width), jnp.bfloat16),
        in_specs=[vmem] * len(operands),
        out_specs=vmem,
        compiler_params=pltpu.CompilerParams(vmem_limit_bytes=4 << 20),
        name="mix",
    )(*operands)


def attend_kept(query, past, lens, step_pairs):
    layers, reqs, steps, heads, flat = query.shape
    width = past.shape[-1] // 2
    scale = 1.0 / math.sqrt(width)
    shaped = query.reshape(layers, reqs, steps, heads, flat // width, width)
    score_past = scale * jnp.einsum(
        "lrnhgd,lrphd->lrhngp", shaped, past[..., :width], preferred_element_type=jnp.float32
    )
    score_step = scale * jnp.einsum(
        "lrnhgd,lrmhd->lrhngm", shaped, step_pairs[..., :width], preferred_element_type=jnp.float32
    )
    filled = jnp.arange(past.shape[2], dtype=jnp.int32)[None, :] < lens[:, None]
    turn = jnp.arange(steps, dtype=jnp.int32)
    score_past = jnp.where(filled[None, :, None, None, None, :], score_past, NEG)
    score_step = jnp.where(
        (turn[:, None] >= turn[None, :])[None, None, None, :, None, :], score_step, NEG
    )
    top = jnp.maximum(
        jnp.max(score_past, axis=-1, keepdims=True), jnp.max(score_step, axis=-1, keepdims=True)
    )
    exp_past = jnp.exp(score_past - top)
    exp_step = jnp.exp(score_step - top)
    total = jnp.sum(exp_past, axis=-1, keepdims=True) + jnp.sum(exp_step, axis=-1, keepdims=True)
    mixed = jnp.einsum(
        "lrhngp,lrphd->lrhngd",
        exp_past.astype(jnp.bfloat16),
        past[..., width:],
        preferred_element_type=jnp.float32,
    ) + jnp.einsum(
        "lrhngm,lrmhd->lrhngd",
        exp_step.astype(jnp.bfloat16),
        step_pairs[..., width:],
        preferred_element_type=jnp.float32,
    )
    return mixed, top, total


def meet_local(
    handoff,
    norm_gain,
    kv_weight,
    span_start,
    token_owner,
    token_slot,
    kv_cache,
    cache_lens,
    step_kv,
    queries,
):
    sizes = (lax.axis_size("group"), lax.axis_size("seq"), lax.axis_size("tp"))
    sections = lax.axis_size("section")
    g = lax.axis_index("group")
    q = lax.axis_index("seq")
    t = lax.axis_index("tp")
    weight = kv_weight[0]
    depth = weight.shape[0] // sizes[0]
    width = weight.shape[2] // 2
    first = depth // 8
    block = handoff[0]
    tokens = block.shape[0]

    code = token_owner[0, :, 0] * 2 + token_slot[0]
    where = jnp.stack([span_start[0] // 64, span_start[0] % 64])
    notes = jnp.concatenate([code, where, jnp.zeros((4 * width - tokens - 2,), jnp.int32)])
    notes = notes.astype(jnp.float32)[None]

    rows4 = weight.reshape(weight.shape[0], 2, 2, width).transpose(0, 2, 1, 3).reshape(-1, width)
    group = g.astype(jnp.int32)[None]
    quarter = (q * sizes[0] + g).astype(jnp.int32)[None]
    (head_start,) = split_heads(
        rows4, norm_gain, group, quarter, depth, 0, first, 1, 1, notes
    )
    start_got = passed_along(head_start, "section", -1)

    cuts = ((False, 0, depth), (True, 0, depth))
    near, far = cut_columns(after(block, head_start), group, depth, cuts)
    near_got = steered(near, lambda a, b, c: (a, c, b), sizes)
    far_got = steered(far, lambda a, b, c: (sizes[0] - 1 - a, c, b), sizes)

    keys_rest, values_rest = split_heads(
        after(rows4, near), norm_gain, group, quarter, depth, first, depth - first, 7, 2
    )
    keys_got = passed_along(keys_rest, "section", -1)
    values_got = passed_along(after(values_rest, start_got), "section", -1)

    near_mate = swapped(near_got)
    far_mate = swapped(far_got)
    same = (q == t).astype(jnp.int32)[None]

    wide = after(block, near_got).astype(jnp.float32)
    square = jnp.sum(wide * wide, axis=-1)[None]
    square = square + swapped(square)

    notes = start_got[first].astype(jnp.int32)
    code = notes[None, :tokens]
    begin = notes[tokens] * 64 + notes[tokens + 1]
    positions = begin + q * tokens + jnp.arange(tokens, dtype=jnp.int32)
    half = width // 2
    freq = jnp.exp(-(jnp.arange(half, dtype=jnp.float32) * 2.0 / width) * math.log(THETA))
    angle = positions.astype(jnp.float32)[:, None] * freq[None, :]
    cosine = jnp.cos(angle)
    sine = jnp.sin(angle)

    query = after(queries[0, 0], near_got)
    layers, reqs, steps, heads, flat = query.shape
    rows = reqs * steps * flat // width
    asked = query.reshape(layers, reqs, steps, heads, flat // width, width)
    asked = asked.transpose(0, 3, 1, 2, 4, 5).reshape(layers, heads, rows, width)
    asked = lax.all_to_all(
        jnp.roll(asked, -1, axis=0), "section", split_axis=0, concat_axis=0, tiled=True
    )
    mixed, top, total = attend_kept(query, kv_cache[0, 0], cache_lens[0, 0], step_kv[0, 0])
    near_mate = after(near_mate, (cosine, sine, code, square, mixed, top, total))

    keys_w = (start_got, keys_got)
    values_w = (start_got, values_got)
    near_pair = ((near_got,), (near_mate,))
    near_part = partial_products(same, (near_pair,), keys_w, 0, 2 * width, 0)
    far_mate = after(far_mate, near_part)
    far_pair = ((far_got,), (far_mate,))
    far_part = partial_products(same, (far_pair,), keys_w, 0, 2 * width, 2)
    keys = summed_over_chips(near_part + far_part, sizes)
    values = summed_over_chips(
        partial_products(same, (near_pair, far_pair), values_w, 2 * width, 2 * width, 0), sizes
    )
    features = block.shape[1] * sizes[2]
    weights, marks = weigh(asked, keys, square, cosine, sine, code, features)
    routed = mix(weights, marks, values, layers)
    routed = lax.all_to_all(routed, "section", split_axis=0, concat_axis=0, tiled=True)
    routed = jnp.roll(routed, 1, axis=0)
    routed = routed.reshape(layers, heads, reqs, steps, flat // width, 2 * width)
    routed = routed.transpose(0, 2, 1, 3, 4, 5).astype(jnp.float32)
    level = jnp.sum(routed[..., width : width + 3], axis=-1, keepdims=True)
    peak = jnp.maximum(level, top)
    kept_part = jnp.exp(top - peak)
    routed_part = jnp.exp(level - peak)
    result = (mixed * kept_part + routed[..., :width] * routed_part) / (
        total * kept_part + routed_part
    )
    result = result.astype(jnp.bfloat16).transpose(0, 1, 3, 2, 4, 5)
    return result.reshape(layers, reqs, steps, heads, flat)[None, None]


def solution(mesh):
    shape = mesh.shape
    body = meet_local if shape["group"] == shape["seq"] == shape["tp"] == 2 else local
    return jax.shard_map(
        body,
        mesh=mesh,
        in_specs=(
            P(("group", "section"), "seq", "tp"),
            P("section", None),
            P("section", "seq", "tp", None),
            P(("group", "section")),
            P(("group", "section"), "seq", None),
            P(("group", "section"), "seq"),
            P(("group", "section"), "seq", None, None, None, "tp", None),
            P(("group", "section"), "seq", None),
            P(("group", "section"), "seq", None, None, None, "tp", None),
            P(("group", "section"), "seq", None, None, None, "tp", None),
        ),
        out_specs=P(("group", "section"), "seq", None, None, None, "tp", None),
        check_vma=False,
    )
```

```python
import math

import jax
import jax.numpy as jnp
from jax import lax
from jax.experimental import pallas as pl
from jax.experimental.pallas import tpu as pltpu
from jax.sharding import PartitionSpec as P

EPS = 1e-05
THETA = 500000.0
NEG = -1e30


def passed_along(value, axis, by):
    length = lax.axis_size(axis)
    return lax.ppermute(value, axis, [(i, (i + by) % length) for i in range(length)])


def rotate(pairs, positions):
    width = pairs.shape[-1] // 2
    half = width // 2
    freq = jnp.exp(-(jnp.arange(half, dtype=jnp.float32) * 2.0 / width) * math.log(THETA))
    angle = positions.astype(jnp.float32)[:, None, None] * freq[None, None, :]
    cosine = jnp.cos(angle)
    sine = jnp.sin(angle)
    first = pairs[..., :half]
    second = pairs[..., half:width]
    turned = jnp.concatenate(
        [first * cosine - second * sine, second * cosine + first * sine], axis=-1
    )
    return jnp.concatenate([turned, pairs[..., width:]], axis=-1)


def attend(query, past, lens, route_pairs, route_mask, step_pairs):
    reqs, steps, heads, flat = query.shape
    width = past.shape[-1] // 2
    groups = flat // width
    scale = 1.0 / math.sqrt(width)
    shaped = query.reshape(reqs, steps, heads, groups, width)
    score_past = (
        jnp.einsum(
            "rnhgd,rphd->rnhgp", shaped, past[..., :width], preferred_element_type=jnp.float32
        )
        * scale
    )
    score_route = (
        jnp.einsum(
            "rnhgd,khd->rnhgk", shaped, route_pairs[..., :width], preferred_element_type=jnp.float32
        )
        * scale
    )
    score_step = (
        jnp.einsum(
            "rnhgd,rmhd->rnhgm", shaped, step_pairs[..., :width], preferred_element_type=jnp.float32
        )
        * scale
    )
    past_mask = jnp.arange(past.shape[1], dtype=jnp.int32)[None, :] < lens[:, None]
    step_mask = (
        jnp.arange(steps, dtype=jnp.int32)[:, None] >= jnp.arange(steps, dtype=jnp.int32)[None, :]
    )
    score_past = jnp.where(past_mask[:, None, None, None, :], score_past, -jnp.inf)
    score_route = jnp.where(route_mask[:, None, None, None, :], score_route, -jnp.inf)
    score_step = jnp.where(step_mask[None, :, None, None, :], score_step, -jnp.inf)
    top = jnp.maximum(
        jnp.maximum(
            jnp.max(score_past, axis=-1, keepdims=True),
            jnp.max(score_route, axis=-1, keepdims=True),
        ),
        jnp.max(score_step, axis=-1, keepdims=True),
    )
    exp_past = jnp.exp(score_past - top)
    exp_route = jnp.exp(score_route - top)
    exp_step = jnp.exp(score_step - top)
    total = (
        jnp.sum(exp_past, axis=-1, keepdims=True)
        + jnp.sum(exp_route, axis=-1, keepdims=True)
        + jnp.sum(exp_step, axis=-1, keepdims=True)
    )
    w_past = (exp_past / total).astype(jnp.bfloat16)
    w_route = (exp_route / total).astype(jnp.bfloat16)
    w_step = (exp_step / total).astype(jnp.bfloat16)
    result = jnp.einsum(
        "rnhgp,rphd->rnhgd", w_past, past[..., width:], preferred_element_type=jnp.float32
    )
    result = result + jnp.einsum(
        "rnhgk,khd->rnhgd", w_route, route_pairs[..., width:], preferred_element_type=jnp.float32
    )
    result = result + jnp.einsum(
        "rnhgm,rmhd->rnhgd", w_step, step_pairs[..., width:], preferred_element_type=jnp.float32
    )
    return result.astype(jnp.bfloat16).reshape(reqs, steps, heads, flat)


def local(
    handoff,
    norm_gain,
    kv_weight,
    span_start,
    token_owner,
    token_slot,
    kv_cache,
    cache_lens,
    step_kv,
    queries,
):
    received = passed_along(handoff, "section", 1)
    whole = lax.all_gather(received[0], "tp", axis=1, tiled=True)
    tokens = whole.shape[0]
    values = whole.astype(jnp.float32)
    meansq = jnp.mean(values * values, axis=-1, keepdims=True)
    normed = (values * lax.rsqrt(meansq + EPS) * norm_gain[0][None, :]).astype(jnp.bfloat16)
    weight = kv_weight[0]
    local_heads = weight.shape[1]
    pair_width = weight.shape[2]
    columns_out = local_heads * pair_width
    piece = lax.all_gather(weight, "seq", axis=0, tiled=True)
    projected = jnp.dot(
        normed, piece.reshape(piece.shape[0], columns_out), preferred_element_type=jnp.float32
    )
    positions = span_start[0] + lax.axis_index("seq") * tokens + jnp.arange(tokens, dtype=jnp.int32)
    prompt_kv = rotate(projected.reshape(tokens, local_heads, pair_width), positions).astype(
        jnp.bfloat16
    )
    sections = lax.axis_size("section")
    capacity = 2 * tokens // sections
    owner = token_owner[0, :, 0]
    slot = token_slot[0]
    onehot = (owner[:, None] == jnp.arange(sections, dtype=jnp.int32)[None, :]).astype(jnp.bfloat16)
    lower = (
        jnp.arange(tokens, dtype=jnp.int32)[:, None] >= jnp.arange(tokens, dtype=jnp.int32)[None, :]
    ).astype(jnp.bfloat16)
    running = jnp.dot(lower, onehot, preferred_element_type=jnp.float32)
    rank = (jnp.sum(running * onehot.astype(jnp.float32), axis=1) - 1.0).astype(jnp.int32)
    place = owner * capacity + rank
    select = (place[:, None] == jnp.arange(sections * capacity, dtype=jnp.int32)[None, :]).astype(
        jnp.bfloat16
    )
    packed = jnp.einsum(
        "ts,tc->sc",
        select,
        prompt_kv.reshape(tokens, columns_out),
        preferred_element_type=jnp.float32,
    )
    packed = packed.astype(jnp.bfloat16).reshape(sections, capacity, local_heads, pair_width)
    labels = jnp.einsum(
        "ts,t->s", select, (slot + 1).astype(jnp.bfloat16), preferred_element_type=jnp.float32
    )
    labels = labels.astype(jnp.bfloat16).reshape(sections, capacity)
    routed, routed_labels = (
        lax.all_to_all(packed, "section", split_axis=0, concat_axis=0, tiled=True),
        lax.all_to_all(labels, "section", split_axis=0, concat_axis=0, tiled=True),
    )
    request_ids = (jnp.arange(kv_cache.shape[3], dtype=jnp.int32) + 1).astype(jnp.float32)
    route_mask = routed_labels.astype(jnp.float32)[:, None, :] == request_ids[None, :, None]
    layered = jax.vmap(attend, in_axes=(0, 0, None, 0, 0, 0))
    result = layered(
        queries[0, 0], kv_cache[0, 0], cache_lens[0, 0], routed, route_mask, step_kv[0, 0]
    )
    return result[None, None]


def steered(value, pairs_of, sizes):
    groups, seqs, cores = sizes
    pairs = []
    for g in range(groups):
        for q in range(seqs):
            for t in range(cores):
                a, b, c = pairs_of(g, q, t)
                pairs.append(((g * seqs + q) * cores + t, (a * seqs + b) * cores + c))
    return lax.ppermute(value, ("group", "seq", "tp"), pairs)


def swapped(value):
    return lax.ppermute(value, "tp", [(0, 1), (1, 0)])


def spread(pieces):
    return [pieces[0]] + [
        lax.ppermute(piece, "section", [(i, i ^ n) for i in range(len(pieces))])
        for n, piece in enumerate(pieces)
        if n
    ]


def after(value, early):
    return lax.optimization_barrier((value, early))[0]


def scaled_heads(wide, gain, tall, width):
    gains = jnp.concatenate(
        [
            jnp.broadcast_to(gain[:, b * width : (b + 1) * width], (width, width)).T
            for b in range(tall // width)
        ],
        axis=0,
    )
    return [
        (wide[pl.ds(n, tall, stride=4), :] * gains).astype(jnp.bfloat16) for n in range(4)
    ]


def split_heads(rows4, gain, group, quarter, depth, start, count, blocks):
    width = rows4.shape[1]
    tall = count // blocks

    def body(group_ref, quarter_ref, mixed_ref, gain_ref, key_ref, value_ref, wide):
        wide[...] = mixed_ref[...].astype(jnp.float32)
        parts = scaled_heads(wide, gain_ref[...], tall, width)
        for head in range(2):
            key_ref[:, head * width : (head + 1) * width] = parts[head]
            value_ref[:, head * width : (head + 1) * width] = parts[2 + head]

    return pl.pallas_call(
        body,
        out_shape=[jax.ShapeDtypeStruct((count, 2 * width), jnp.bfloat16)] * 2,
        grid_spec=pltpu.PrefetchScalarGridSpec(
            num_scalar_prefetch=2,
            grid=(blocks,),
            in_specs=[
                pl.BlockSpec(
                    (4 * tall, width),
                    lambda i, group, quarter: (group[0] * (depth // tall) + start // tall + i, 0),
                ),
                pl.BlockSpec(
                    (1, tall),
                    lambda i, group, quarter: (0, quarter[0] * (depth // tall) + start // tall + i),
                ),
            ],
            out_specs=[pl.BlockSpec((tall, 2 * width), lambda i, group, quarter: (i, 0))] * 2,
            scratch_shapes=[pltpu.VMEM((4 * tall, width), jnp.float32)],
        ),
        compiler_params=pltpu.CompilerParams(vmem_limit_bytes=57 << 20),
        name="split_heads",
    )(group, quarter, rows4, gain)


def prepare(block, rows4, gain, group, quarter, owner, slot, begin, depth, first):
    tokens = block.shape[0]
    width = rows4.shape[1]
    extra = 16

    def body(
        group_ref,
        quarter_ref,
        begin_ref,
        owner_ref,
        slot_ref,
        block_ref,
        rows_ref,
        gain_ref,
        head_ref,
        near_ref,
        far_ref,
        mixed,
        wide,
        gains,
        sems,
    ):
        row = pl.multiple_of(group_ref[0] * (4 * depth), 4 * depth)
        lane = pl.multiple_of(quarter_ref[0] * depth, depth)
        loads = [
            pltpu.make_async_copy(rows_ref.at[pl.ds(row, 4 * first), :], mixed, sems.at[0]),
            pltpu.make_async_copy(gain_ref.at[:, pl.ds(lane, first)], gains, sems.at[1]),
        ]
        for n, ref in enumerate((near_ref, far_ref)):
            which = group_ref[0] if n == 0 else 1 - group_ref[0]
            column = pl.multiple_of(which * depth, depth)
            loads.append(
                pltpu.make_async_copy(
                    block_ref.at[:, pl.ds(column, depth)], ref, sems.at[2 + n]
                )
            )
        for copy in loads:
            copy.start()
        loads[0].wait()
        loads[1].wait()
        wide[...] = mixed[...].astype(jnp.float32)
        for n, part in enumerate(scaled_heads(wide, gains[...], first, width)):
            head_ref[:first, n * width : (n + 1) * width] = part
        code = (owner_ref[...] * 2 + slot_ref[...]).astype(jnp.float32)
        start = begin_ref[0]
        high = start // 64
        mark = lax.broadcasted_iota(jnp.int32, (1, 4 * width - tokens), 1)
        mark = jnp.where(mark == 0, high, jnp.where(mark == 1, start - high * 64, 0))
        head_ref[first:, :tokens] = jnp.broadcast_to(code, (extra, tokens)).astype(jnp.bfloat16)
        head_ref[first:, tokens:] = jnp.broadcast_to(
            mark.astype(jnp.float32), (extra, 4 * width - tokens)
        ).astype(jnp.bfloat16)
        loads[2].wait()
        loads[3].wait()

    smem = pl.BlockSpec(memory_space=pltpu.SMEM)
    vmem = pl.BlockSpec(memory_space=pltpu.VMEM)
    hbm = pl.BlockSpec(memory_space=pl.ANY)
    return pl.pallas_call(
        body,
        out_shape=[jax.ShapeDtypeStruct((first + extra, 4 * width), jnp.bfloat16)]
        + [jax.ShapeDtypeStruct((tokens, depth), jnp.bfloat16)] * 2,
        in_specs=[smem, smem, smem, vmem, vmem, hbm, hbm, hbm],
        out_specs=[vmem, vmem, vmem],
        scratch_shapes=[
            pltpu.VMEM((4 * first, width), jnp.bfloat16),
            pltpu.VMEM((4 * first, width), jnp.float32),
            pltpu.VMEM((1, first), jnp.float32),
            pltpu.SemaphoreType.DMA((4,)),
        ],
        compiler_params=pltpu.CompilerParams(vmem_limit_bytes=60 << 20),
        name="prepare",
    )(group, quarter, begin, owner, slot, block, rows4, gain)


def partial_products(same, pairs, weights, first_column, columns, first_kind):
    tokens = pairs[0][0][0].shape[0]
    depth = pairs[0][0][0].shape[1]
    acts = [piece for pair in pairs for side in pair for piece in side]
    count = len(acts) + len(weights)

    def body(same_ref, *refs):
        act_refs = refs[: len(acts)]
        weight_refs = refs[len(acts) : count]
        outs = refs[count : count + 2 * len(pairs)]
        held, weight, sems = refs[count + 2 * len(pairs) :]
        weight_copies = []
        row = 0
        for n, ref in enumerate(weight_refs):
            taken = min(ref.shape[0], depth - row) // 128 * 128
            column = first_column if ref.shape[1] > columns else 0
            weight_copies.append(
                pltpu.make_async_copy(
                    ref.at[pl.ds(0, taken), pl.ds(column, columns)],
                    weight.at[pl.ds(row, taken), :],
                    sems.at[len(acts) + n],
                )
            )
            row += taken
        for copy in weight_copies:
            copy.start()
        act_copies = []
        n = 0
        for p, pair in enumerate(pairs):
            mine = []
            for side in range(2):
                slot = 2 * p + ((1 - same_ref[0]) if side == 0 else same_ref[0])
                column = 0
                for piece in pair[side]:
                    wide = piece.shape[1]
                    copy = pltpu.make_async_copy(
                        act_refs[n], held.at[slot, :, pl.ds(column, wide)], sems.at[n]
                    )
                    copy.start()
                    mine.append(copy)
                    column += wide
                    n += 1
            act_copies.append(mine)
        for copy in weight_copies:
            copy.wait()
        for p in range(len(pairs)):
            for copy in act_copies[p]:
                copy.wait()
            for side in range(2):
                out = outs[2 * p + side]
                out[...] = jnp.dot(
                    held[2 * p + side], weight[...], preferred_element_type=jnp.float32
                ).astype(out.dtype)

    anywhere = pl.BlockSpec(memory_space=pl.ANY)
    vmem = pl.BlockSpec(memory_space=pltpu.VMEM)
    kinds = [jnp.float32, jnp.bfloat16, jnp.bfloat16, jnp.bfloat16]
    kinds = kinds[first_kind : first_kind + 2 * len(pairs)]
    return pl.pallas_call(
        body,
        out_shape=[jax.ShapeDtypeStruct((tokens, columns), kind) for kind in kinds],
        in_specs=[pl.BlockSpec(memory_space=pltpu.SMEM)] + [anywhere] * count,
        out_specs=[vmem] * len(kinds),
        scratch_shapes=[
            pltpu.VMEM((2 * len(pairs), tokens, depth), jnp.bfloat16),
            pltpu.VMEM((depth, columns), jnp.bfloat16),
            pltpu.SemaphoreType.DMA((count,)),
        ],
        compiler_params=pltpu.CompilerParams(vmem_limit_bytes=(5 + 4 * len(pairs)) << 20),
        name="partial_products",
    )(same, *acts, *weights)


def summed_over_chips(parts, sizes):
    own, across, far, far_across = parts
    groups, seqs, _ = sizes
    return (
        own,
        steered(across, lambda g, q, t: (g, seqs - 1 - q, t), sizes),
        steered(far, lambda g, q, t: (groups - 1 - g, q, t), sizes),
        steered(far_across, lambda g, q, t: (groups - 1 - g, seqs - 1 - q, t), sizes),
    )


def weigh(section, asked, keys, squares, cosine, sine, code, features):
    owners = len(asked)
    heads, rows, width = asked[0].shape
    tokens = code.shape[1]
    half = width // 2
    requests = 2
    factor = 1.0 / math.sqrt(width)
    span = owners * rows

    def body(section_ref, *refs):
        asked_refs, rest = refs[:owners], refs[owners:]
        key_refs = rest[:4]
        one_ref, two_ref, cos_ref, sin_ref, code_ref, weight_ref, mark_ref = rest[4:]
        scale = lax.rsqrt((one_ref[...] + two_ref[...]) / features + EPS)
        place = lax.broadcasted_iota(jnp.int32, (span, tokens), 0)
        owner = (place // rows) ^ section_ref[0]
        request = owner * requests + place % rows // (rows // requests)
        mine = request == code_ref[...]
        lane = lax.broadcasted_iota(jnp.int32, (span, width), 1)
        for h in range(heads):
            columns = slice(h * width, (h + 1) * width)
            key = key_refs[0][:, columns]
            for ref in key_refs[1:]:
                key = key + ref[:, columns].astype(jnp.float32)
            first = key[:, :half]
            second = key[:, half:]
            key = jnp.concatenate(
                [
                    first * cos_ref[...] - second * sin_ref[...],
                    second * cos_ref[...] + first * sin_ref[...],
                ],
                axis=1,
            ).astype(jnp.bfloat16)
            query = jnp.concatenate([ref[h] for ref in asked_refs], axis=0)
            score = lax.dot_general(
                query, key, (((1,), (1,)), ((), ())), preferred_element_type=jnp.float32
            ) * (scale * factor)
            score = jnp.where(mine, score, NEG)
            top = jnp.max(score, axis=1, keepdims=True)
            weight = jnp.where(mine, jnp.exp(score - top), 0.0)
            total = jnp.sum(weight, axis=1, keepdims=True)
            some = total > 0.0
            safe = jnp.where(some, total, 1.0)
            weight_ref[h] = (weight / safe * scale).astype(jnp.bfloat16)
            level = jnp.where(some, top + jnp.log(safe), NEG)
            high = level.astype(jnp.bfloat16).astype(jnp.float32)
            middle = (level - high).astype(jnp.bfloat16).astype(jnp.float32)
            low = level - high - middle
            mark_ref[h] = jnp.where(
                lane == 0, high, jnp.where(lane == 1, middle, jnp.where(lane == 2, low, 0.0))
            ).astype(jnp.bfloat16)

    vmem = pl.BlockSpec(memory_space=pltpu.VMEM)
    operands = (*asked, *keys, *squares, cosine, sine, code)
    return pl.pallas_call(
        body,
        out_shape=[
            jax.ShapeDtypeStruct((heads, span, tokens), jnp.bfloat16),
            jax.ShapeDtypeStruct((heads, span, width), jnp.bfloat16),
        ],
        in_specs=[pl.BlockSpec(memory_space=pltpu.SMEM)] + [vmem] * len(operands),
        out_specs=[vmem] * 2,
        compiler_params=pltpu.CompilerParams(vmem_limit_bytes=6 << 20),
        name="weigh",
    )(section, *operands)


def mix(weights, marks, values, owners):
    heads, span, _ = weights.shape
    width = marks.shape[2]
    rows = span // owners

    def body(weight_ref, mark_ref, *rest):
        value_refs, outs = rest[: len(values)], rest[len(values) :]
        for h in range(heads):
            columns = slice(h * width, (h + 1) * width)
            value = value_refs[0][:, columns]
            for ref in value_refs[1:]:
                value = value + ref[:, columns].astype(jnp.float32)
            mixed = jnp.dot(
                weight_ref[h], value.astype(jnp.bfloat16), preferred_element_type=jnp.float32
            ).astype(jnp.bfloat16)
            for step in range(owners):
                outs[step][h, :, :width] = mixed[step * rows : (step + 1) * rows]
                outs[step][h, :, width:] = mark_ref[h, step * rows : (step + 1) * rows, :]

    vmem = pl.BlockSpec(memory_space=pltpu.VMEM)
    operands = (weights, marks, *values)
    return pl.pallas_call(
        body,
        out_shape=[jax.ShapeDtypeStruct((heads, rows, 2 * width), jnp.bfloat16)] * owners,
        in_specs=[vmem] * len(operands),
        out_specs=[vmem] * owners,
        compiler_params=pltpu.CompilerParams(vmem_limit_bytes=4 << 20),
        name="mix",
    )(*operands)


def merge(section, pieces, mixed, levels):
    layers, spans, width = mixed.shape
    heads, rows, _ = pieces[0].shape

    def body(section_ref, *rest):
        piece_refs = rest[: len(pieces)]
        mixed_ref, level_ref, out_ref = rest[len(pieces) :]
        for step, ref in enumerate(piece_refs):
            layer = ((section_ref[0] ^ step) + 1) % layers
            routed = jnp.concatenate([ref[h] for h in range(heads)], axis=0)
            level = jnp.sum(
                routed[:, width : width + 3].astype(jnp.float32), axis=1, keepdims=True
            )
            high = level_ref[layer]
            peak = jnp.maximum(level, high)
            kept = jnp.exp(high - peak)
            other = jnp.exp(level - peak)
            share = 1.0 / (kept + other)
            out_ref[layer] = (
                mixed_ref[layer] * (kept * share)
                + routed[:, :width].astype(jnp.float32) * (other * share)
            ).astype(jnp.bfloat16)

    vmem = pl.BlockSpec(memory_space=pltpu.VMEM)
    operands = (*pieces, mixed, levels)
    return pl.pallas_call(
        body,
        out_shape=jax.ShapeDtypeStruct((layers, spans, width), jnp.bfloat16),
        in_specs=[pl.BlockSpec(memory_space=pltpu.SMEM)] + [vmem] * len(operands),
        out_specs=vmem,
        compiler_params=pltpu.CompilerParams(vmem_limit_bytes=6 << 20),
        name="merge",
    )(section, *operands)


def keep(asked, cache, recent, lens, steps):
    layers, heads, rows, width = asked.shape
    reqs = lens.shape[0]
    filled = cache.shape[2] // reqs
    factor = 1.0 / math.sqrt(width)
    lane = (((1,), (1,)), ((), ()))

    def body(lens_ref, asked_ref, cache_ref, recent_ref, kept_ref, level_ref):
        row = lax.broadcasted_iota(jnp.int32, (rows, reqs * filled), 0)
        column = lax.broadcasted_iota(jnp.int32, (rows, reqs * filled), 1)
        own = row // (rows // reqs)
        length = lens_ref[reqs - 1]
        for r in reversed(range(reqs - 1)):
            length = jnp.where(own == r, lens_ref[r], length)
        old = (column // filled == own) & (column % filled < length)
        row = lax.broadcasted_iota(jnp.int32, (rows, reqs * steps), 0)
        column = lax.broadcasted_iota(jnp.int32, (rows, reqs * steps), 1)
        turn = row % (rows // reqs) // (rows // reqs // steps)
        new = (column // steps == row // (rows // reqs)) & (column % steps <= turn)
        for l in range(layers):
            for h in range(heads):
                query = asked_ref[l, h]
                past = cache_ref[l, h]
                step = recent_ref[l, h]
                score_old = factor * lax.dot_general(
                    query, past[:, :width], lane, preferred_element_type=jnp.float32
                )
                score_new = factor * lax.dot_general(
                    query, step[:, :width], lane, preferred_element_type=jnp.float32
                )
                score_old = jnp.where(old, score_old, NEG)
                score_new = jnp.where(new, score_new, NEG)
                top = jnp.maximum(
                    jnp.max(score_old, axis=1, keepdims=True),
                    jnp.max(score_new, axis=1, keepdims=True),
                )
                weight_old = jnp.exp(score_old - top)
                weight_new = jnp.exp(score_new - top)
                total = jnp.sum(weight_old, axis=1, keepdims=True) + jnp.sum(
                    weight_new, axis=1, keepdims=True
                )
                mixed = jnp.dot(
                    weight_old.astype(jnp.bfloat16),
                    past[:, width:],
                    preferred_element_type=jnp.float32,
                ) + jnp.dot(
                    weight_new.astype(jnp.bfloat16),
                    step[:, width:],
                    preferred_element_type=jnp.float32,
                )
                kept_ref[l, h * rows : (h + 1) * rows, :] = mixed / total
                level_ref[l, h * rows : (h + 1) * rows, :] = jnp.broadcast_to(
                    top + jnp.log(total), (rows, width)
                )

    vmem = pl.BlockSpec(memory_space=pltpu.VMEM)
    return pl.pallas_call(
        body,
        out_shape=[jax.ShapeDtypeStruct((layers, heads * rows, width), jnp.float32)] * 2,
        in_specs=[pl.BlockSpec(memory_space=pltpu.SMEM), vmem, vmem, vmem],
        out_specs=[vmem, vmem],
        compiler_params=pltpu.CompilerParams(vmem_limit_bytes=6 << 20),
        cost_estimate=pl.CostEstimate(flops=40000000000, transcendentals=0, bytes_accessed=1),
        name="keep",
    )(lens, asked, cache, recent)


def meet_local(
    handoff,
    norm_gain,
    kv_weight,
    span_start,
    token_owner,
    token_slot,
    kv_cache,
    cache_lens,
    step_kv,
    queries,
):
    sizes = (lax.axis_size("group"), lax.axis_size("seq"), lax.axis_size("tp"))
    sections = lax.axis_size("section")
    g = lax.axis_index("group")
    q = lax.axis_index("seq")
    t = lax.axis_index("tp")
    weight = kv_weight[0]
    depth = weight.shape[0] // sizes[0]
    width = weight.shape[2] // 2
    first = depth // 8
    block = handoff[0]
    tokens = block.shape[0]

    rows4 = weight.reshape(weight.shape[0], 2, 2, width).transpose(0, 2, 1, 3).reshape(-1, width)
    group = g.astype(jnp.int32)[None]
    quarter = (q * sizes[0] + g).astype(jnp.int32)[None]
    head_start, near, far = prepare(
        block,
        rows4,
        norm_gain,
        group,
        quarter,
        token_owner.reshape(1, tokens),
        token_slot,
        span_start,
        depth,
        first,
    )
    start_got = passed_along(head_start, "section", -1)

    near_got = steered(near, lambda a, b, c: (a, c, b), sizes)
    far_got = steered(far, lambda a, b, c: (sizes[0] - 1 - a, c, b), sizes)

    keys_rest, values_rest = split_heads(
        after(rows4, near), norm_gain, group, quarter, depth, first, depth - first, 7
    )
    keys_got = passed_along(keys_rest, "section", -1)
    values_got = passed_along(after(values_rest, start_got), "section", -1)

    near_mate = swapped(near_got)
    far_mate = swapped(far_got)
    same = (q == t).astype(jnp.int32)[None]

    wide = after(block, near_got).astype(jnp.float32)
    square = jnp.sum(wide * wide, axis=-1)[None]
    squares = (square, swapped(square))

    notes = start_got[first].astype(jnp.int32)
    code = notes[None, :tokens]
    begin = notes[tokens] * 64 + notes[tokens + 1]
    positions = begin + q * tokens + jnp.arange(tokens, dtype=jnp.int32)
    half = width // 2
    freq = jnp.exp(-(jnp.arange(half, dtype=jnp.float32) * 2.0 / width) * math.log(THETA))
    angle = positions.astype(jnp.float32)[:, None] * freq[None, :]
    cosine = jnp.cos(angle)
    sine = jnp.sin(angle)

    query = after(queries[0, 0], near_got)
    layers, reqs, steps, heads, flat = query.shape
    rows = reqs * steps * flat // width
    asked = query.reshape(layers, reqs, steps, heads, flat // width, width)
    asked = asked.transpose(0, 3, 1, 2, 4, 5).reshape(layers, heads, rows, width)
    section = lax.axis_index("section")
    everything = asked
    chosen = [
        lax.dynamic_index_in_dim(everything, ((section ^ n) + 1) % layers, 0, keepdims=False)
        for n in range(layers)
    ]
    cache = kv_cache[0, 0].transpose(0, 3, 1, 2, 4).reshape(layers, heads, -1, 2 * width)
    recent = step_kv[0, 0].transpose(0, 3, 1, 2, 4).reshape(layers, heads, -1, 2 * width)
    kept, levels = keep(everything, cache, recent, cache_lens[0, 0], steps)

    near_mate = after(near_mate, (cosine, sine, code, square, kept, levels, *chosen))
    keys_w = (start_got, keys_got)
    values_w = (start_got, values_got)
    near_pair = ((near_got,), (near_mate,))
    near_part = partial_products(same, (near_pair,), keys_w, 0, 2 * width, 0)
    far_mate = after(far_mate, near_part)
    far_pair = ((far_got,), (far_mate,))
    far_part = partial_products(same, (far_pair,), keys_w, 0, 2 * width, 2)
    keys = summed_over_chips(near_part + far_part, sizes)
    value_parts = partial_products(
        same, (near_pair, far_pair), values_w, 2 * width, 2 * width, 0
    )
    values = summed_over_chips(value_parts, sizes)
    asked = spread(list(after(tuple(chosen), keys[1])))
    features = block.shape[1] * sizes[2]
    here = section.astype(jnp.int32)[None]
    weights, marks = weigh(here, asked, keys, squares, cosine, sine, code, features)
    pieces = spread(mix(weights, marks, values, layers))
    result = merge(here, pieces, kept, levels)
    result = result.reshape(layers, heads, reqs, steps, flat // width, width)
    result = result.transpose(0, 2, 3, 1, 4, 5)
    return result.reshape(layers, reqs, steps, heads, flat)[None, None]


def solution(mesh):
    shape = mesh.shape
    paired = shape["group"] == shape["seq"] == shape["tp"] == 2
    body = meet_local if paired and shape["section"] == 4 else local
    return jax.shard_map(
        body,
        mesh=mesh,
        in_specs=(
            P(("group", "section"), "seq", "tp"),
            P("section", None),
            P("section", "seq", "tp", None),
            P(("group", "section")),
            P(("group", "section"), "seq", None),
            P(("group", "section"), "seq"),
            P(("group", "section"), "seq", None, None, None, "tp", None),
            P(("group", "section"), "seq", None),
            P(("group", "section"), "seq", None, None, None, "tp", None),
            P(("group", "section"), "seq", None, None, None, "tp", None),
        ),
        out_specs=P(("group", "section"), "seq", None, None, None, "tp", None),
        check_vma=False,
    )
```

```python
import math

import jax
import jax.numpy as jnp
from jax import lax
from jax.experimental import pallas as pl
from jax.experimental.pallas import tpu as pltpu
from jax.sharding import PartitionSpec as P

EPS = 1e-05
THETA = 500000.0
NEG = -1e30


def passed_along(value, axis, by):
    length = lax.axis_size(axis)
    return lax.ppermute(value, axis, [(i, (i + by) % length) for i in range(length)])


def rotate(pairs, positions):
    width = pairs.shape[-1] // 2
    half = width // 2
    freq = jnp.exp(-(jnp.arange(half, dtype=jnp.float32) * 2.0 / width) * math.log(THETA))
    angle = positions.astype(jnp.float32)[:, None, None] * freq[None, None, :]
    cosine = jnp.cos(angle)
    sine = jnp.sin(angle)
    first = pairs[..., :half]
    second = pairs[..., half:width]
    turned = jnp.concatenate(
        [first * cosine - second * sine, second * cosine + first * sine], axis=-1
    )
    return jnp.concatenate([turned, pairs[..., width:]], axis=-1)


def attend(query, past, lens, route_pairs, route_mask, step_pairs):
    reqs, steps, heads, flat = query.shape
    width = past.shape[-1] // 2
    groups = flat // width
    scale = 1.0 / math.sqrt(width)
    shaped = query.reshape(reqs, steps, heads, groups, width)
    score_past = (
        jnp.einsum(
            "rnhgd,rphd->rnhgp", shaped, past[..., :width], preferred_element_type=jnp.float32
        )
        * scale
    )
    score_route = (
        jnp.einsum(
            "rnhgd,khd->rnhgk", shaped, route_pairs[..., :width], preferred_element_type=jnp.float32
        )
        * scale
    )
    score_step = (
        jnp.einsum(
            "rnhgd,rmhd->rnhgm", shaped, step_pairs[..., :width], preferred_element_type=jnp.float32
        )
        * scale
    )
    past_mask = jnp.arange(past.shape[1], dtype=jnp.int32)[None, :] < lens[:, None]
    step_mask = (
        jnp.arange(steps, dtype=jnp.int32)[:, None] >= jnp.arange(steps, dtype=jnp.int32)[None, :]
    )
    score_past = jnp.where(past_mask[:, None, None, None, :], score_past, -jnp.inf)
    score_route = jnp.where(route_mask[:, None, None, None, :], score_route, -jnp.inf)
    score_step = jnp.where(step_mask[None, :, None, None, :], score_step, -jnp.inf)
    top = jnp.maximum(
        jnp.maximum(
            jnp.max(score_past, axis=-1, keepdims=True),
            jnp.max(score_route, axis=-1, keepdims=True),
        ),
        jnp.max(score_step, axis=-1, keepdims=True),
    )
    exp_past = jnp.exp(score_past - top)
    exp_route = jnp.exp(score_route - top)
    exp_step = jnp.exp(score_step - top)
    total = (
        jnp.sum(exp_past, axis=-1, keepdims=True)
        + jnp.sum(exp_route, axis=-1, keepdims=True)
        + jnp.sum(exp_step, axis=-1, keepdims=True)
    )
    w_past = (exp_past / total).astype(jnp.bfloat16)
    w_route = (exp_route / total).astype(jnp.bfloat16)
    w_step = (exp_step / total).astype(jnp.bfloat16)
    result = jnp.einsum(
        "rnhgp,rphd->rnhgd", w_past, past[..., width:], preferred_element_type=jnp.float32
    )
    result = result + jnp.einsum(
        "rnhgk,khd->rnhgd", w_route, route_pairs[..., width:], preferred_element_type=jnp.float32
    )
    result = result + jnp.einsum(
        "rnhgm,rmhd->rnhgd", w_step, step_pairs[..., width:], preferred_element_type=jnp.float32
    )
    return result.astype(jnp.bfloat16).reshape(reqs, steps, heads, flat)


def local(
    handoff,
    norm_gain,
    kv_weight,
    span_start,
    token_owner,
    token_slot,
    kv_cache,
    cache_lens,
    step_kv,
    queries,
):
    received = passed_along(handoff, "section", 1)
    whole = lax.all_gather(received[0], "tp", axis=1, tiled=True)
    tokens = whole.shape[0]
    values = whole.astype(jnp.float32)
    meansq = jnp.mean(values * values, axis=-1, keepdims=True)
    normed = (values * lax.rsqrt(meansq + EPS) * norm_gain[0][None, :]).astype(jnp.bfloat16)
    weight = kv_weight[0]
    local_heads = weight.shape[1]
    pair_width = weight.shape[2]
    columns_out = local_heads * pair_width
    piece = lax.all_gather(weight, "seq", axis=0, tiled=True)
    projected = jnp.dot(
        normed, piece.reshape(piece.shape[0], columns_out), preferred_element_type=jnp.float32
    )
    positions = span_start[0] + lax.axis_index("seq") * tokens + jnp.arange(tokens, dtype=jnp.int32)
    prompt_kv = rotate(projected.reshape(tokens, local_heads, pair_width), positions).astype(
        jnp.bfloat16
    )
    sections = lax.axis_size("section")
    capacity = 2 * tokens // sections
    owner = token_owner[0, :, 0]
    slot = token_slot[0]
    onehot = (owner[:, None] == jnp.arange(sections, dtype=jnp.int32)[None, :]).astype(jnp.bfloat16)
    lower = (
        jnp.arange(tokens, dtype=jnp.int32)[:, None] >= jnp.arange(tokens, dtype=jnp.int32)[None, :]
    ).astype(jnp.bfloat16)
    running = jnp.dot(lower, onehot, preferred_element_type=jnp.float32)
    rank = (jnp.sum(running * onehot.astype(jnp.float32), axis=1) - 1.0).astype(jnp.int32)
    place = owner * capacity + rank
    select = (place[:, None] == jnp.arange(sections * capacity, dtype=jnp.int32)[None, :]).astype(
        jnp.bfloat16
    )
    packed = jnp.einsum(
        "ts,tc->sc",
        select,
        prompt_kv.reshape(tokens, columns_out),
        preferred_element_type=jnp.float32,
    )
    packed = packed.astype(jnp.bfloat16).reshape(sections, capacity, local_heads, pair_width)
    labels = jnp.einsum(
        "ts,t->s", select, (slot + 1).astype(jnp.bfloat16), preferred_element_type=jnp.float32
    )
    labels = labels.astype(jnp.bfloat16).reshape(sections, capacity)
    routed, routed_labels = (
        lax.all_to_all(packed, "section", split_axis=0, concat_axis=0, tiled=True),
        lax.all_to_all(labels, "section", split_axis=0, concat_axis=0, tiled=True),
    )
    request_ids = (jnp.arange(kv_cache.shape[3], dtype=jnp.int32) + 1).astype(jnp.float32)
    route_mask = routed_labels.astype(jnp.float32)[:, None, :] == request_ids[None, :, None]
    layered = jax.vmap(attend, in_axes=(0, 0, None, 0, 0, 0))
    result = layered(
        queries[0, 0], kv_cache[0, 0], cache_lens[0, 0], routed, route_mask, step_kv[0, 0]
    )
    return result[None, None]


def steered(value, pairs_of, sizes):
    groups, seqs, cores = sizes
    pairs = []
    for g in range(groups):
        for q in range(seqs):
            for t in range(cores):
                a, b, c = pairs_of(g, q, t)
                pairs.append(((g * seqs + q) * cores + t, (a * seqs + b) * cores + c))
    return lax.ppermute(value, ("group", "seq", "tp"), pairs)


def swapped(value):
    return lax.ppermute(value, "tp", [(0, 1), (1, 0)])


def spread(pieces):
    return [pieces[0]] + [
        lax.ppermute(piece, "section", [(i, i ^ n) for i in range(len(pieces))])
        for n, piece in enumerate(pieces)
        if n
    ]


def after(value, early):
    return lax.optimization_barrier((value, early))[0]


def scaled_heads(wide, gain, tall, width):
    gains = jnp.concatenate(
        [
            jnp.broadcast_to(gain[:, b * width : (b + 1) * width], (width, width)).T
            for b in range(tall // width)
        ],
        axis=0,
    )
    return [
        (wide[pl.ds(n, tall, stride=4), :] * gains).astype(jnp.bfloat16) for n in range(4)
    ]


def split_heads(rows4, gain, group, quarter, depth, start, count, blocks):
    width = rows4.shape[1]
    tall = count // blocks

    def body(group_ref, quarter_ref, mixed_ref, gain_ref, key_ref, value_ref, wide):
        wide[...] = mixed_ref[...].astype(jnp.float32)
        parts = scaled_heads(wide, gain_ref[...], tall, width)
        for head in range(2):
            key_ref[:, head * width : (head + 1) * width] = parts[head]
            value_ref[:, head * width : (head + 1) * width] = parts[2 + head]

    return pl.pallas_call(
        body,
        out_shape=[jax.ShapeDtypeStruct((count, 2 * width), jnp.bfloat16)] * 2,
        grid_spec=pltpu.PrefetchScalarGridSpec(
            num_scalar_prefetch=2,
            grid=(blocks,),
            in_specs=[
                pl.BlockSpec(
                    (4 * tall, width),
                    lambda i, group, quarter: (group[0] * (depth // tall) + start // tall + i, 0),
                ),
                pl.BlockSpec(
                    (1, tall),
                    lambda i, group, quarter: (0, quarter[0] * (depth // tall) + start // tall + i),
                ),
            ],
            out_specs=[pl.BlockSpec((tall, 2 * width), lambda i, group, quarter: (i, 0))] * 2,
            scratch_shapes=[pltpu.VMEM((4 * tall, width), jnp.float32)],
        ),
        compiler_params=pltpu.CompilerParams(vmem_limit_bytes=57 << 20),
        name="split_heads",
    )(group, quarter, rows4, gain)


def prepare(block, rows4, gain, group, quarter, owner, slot, begin, depth, first):
    tokens = block.shape[0]
    width = rows4.shape[1]
    extra = 16

    def body(
        group_ref,
        quarter_ref,
        begin_ref,
        owner_ref,
        slot_ref,
        block_ref,
        rows_ref,
        gain_ref,
        head_ref,
        near_ref,
        far_ref,
        mixed,
        wide,
        gains,
        sems,
    ):
        row = pl.multiple_of(group_ref[0] * (4 * depth), 4 * depth)
        lane = pl.multiple_of(quarter_ref[0] * depth, depth)
        loads = [
            pltpu.make_async_copy(rows_ref.at[pl.ds(row, 4 * first), :], mixed, sems.at[0]),
            pltpu.make_async_copy(gain_ref.at[:, pl.ds(lane, first)], gains, sems.at[1]),
        ]
        for n, ref in enumerate((near_ref, far_ref)):
            which = group_ref[0] if n == 0 else 1 - group_ref[0]
            column = pl.multiple_of(which * depth, depth)
            loads.append(
                pltpu.make_async_copy(
                    block_ref.at[:, pl.ds(column, depth)], ref, sems.at[2 + n]
                )
            )
        for copy in loads:
            copy.start()
        loads[0].wait()
        loads[1].wait()
        wide[...] = mixed[...].astype(jnp.float32)
        for n, part in enumerate(scaled_heads(wide, gains[...], first, width)):
            head_ref[:first, n * width : (n + 1) * width] = part
        code = (owner_ref[...] * 2 + slot_ref[...]).astype(jnp.float32)
        start = begin_ref[0]
        high = start // 64
        mark = lax.broadcasted_iota(jnp.int32, (1, 4 * width - tokens), 1)
        mark = jnp.where(mark == 0, high, jnp.where(mark == 1, start - high * 64, 0))
        head_ref[first:, :tokens] = jnp.broadcast_to(code, (extra, tokens)).astype(jnp.bfloat16)
        head_ref[first:, tokens:] = jnp.broadcast_to(
            mark.astype(jnp.float32), (extra, 4 * width - tokens)
        ).astype(jnp.bfloat16)
        loads[2].wait()
        loads[3].wait()

    smem = pl.BlockSpec(memory_space=pltpu.SMEM)
    vmem = pl.BlockSpec(memory_space=pltpu.VMEM)
    hbm = pl.BlockSpec(memory_space=pl.ANY)
    return pl.pallas_call(
        body,
        out_shape=[jax.ShapeDtypeStruct((first + extra, 4 * width), jnp.bfloat16)]
        + [jax.ShapeDtypeStruct((tokens, depth), jnp.bfloat16)] * 2,
        in_specs=[smem, smem, smem, vmem, vmem, hbm, hbm, hbm],
        out_specs=[vmem, vmem, vmem],
        scratch_shapes=[
            pltpu.VMEM((4 * first, width), jnp.bfloat16),
            pltpu.VMEM((4 * first, width), jnp.float32),
            pltpu.VMEM((1, first), jnp.float32),
            pltpu.SemaphoreType.DMA((4,)),
        ],
        compiler_params=pltpu.CompilerParams(vmem_limit_bytes=60 << 20),
        name="prepare",
    )(group, quarter, begin, owner, slot, block, rows4, gain)


def partial_products(same, pairs, weights, first_column, columns, first_kind):
    tokens = pairs[0][0][0].shape[0]
    depth = pairs[0][0][0].shape[1]
    acts = [piece for pair in pairs for side in pair for piece in side]
    count = len(acts) + len(weights)

    def body(same_ref, *refs):
        act_refs = refs[: len(acts)]
        weight_refs = refs[len(acts) : count]
        outs = refs[count : count + 2 * len(pairs)]
        held, weight, sems = refs[count + 2 * len(pairs) :]
        weight_copies = []
        row = 0
        for n, ref in enumerate(weight_refs):
            taken = min(ref.shape[0], depth - row) // 128 * 128
            column = first_column if ref.shape[1] > columns else 0
            weight_copies.append(
                pltpu.make_async_copy(
                    ref.at[pl.ds(0, taken), pl.ds(column, columns)],
                    weight.at[pl.ds(row, taken), :],
                    sems.at[len(acts) + n],
                )
            )
            row += taken
        for copy in weight_copies:
            copy.start()
        act_copies = []
        n = 0
        for p, pair in enumerate(pairs):
            mine = []
            for side in range(2):
                slot = 2 * p + ((1 - same_ref[0]) if side == 0 else same_ref[0])
                column = 0
                for piece in pair[side]:
                    wide = piece.shape[1]
                    copy = pltpu.make_async_copy(
                        act_refs[n], held.at[slot, :, pl.ds(column, wide)], sems.at[n]
                    )
                    copy.start()
                    mine.append(copy)
                    column += wide
                    n += 1
            act_copies.append(mine)
        for copy in weight_copies:
            copy.wait()
        for p in range(len(pairs)):
            for copy in act_copies[p]:
                copy.wait()
            for side in range(2):
                out = outs[2 * p + side]
                out[...] = jnp.dot(
                    held[2 * p + side], weight[...], preferred_element_type=jnp.float32
                ).astype(out.dtype)

    anywhere = pl.BlockSpec(memory_space=pl.ANY)
    vmem = pl.BlockSpec(memory_space=pltpu.VMEM)
    kinds = [jnp.float32, jnp.bfloat16, jnp.bfloat16, jnp.bfloat16]
    kinds = kinds[first_kind : first_kind + 2 * len(pairs)]
    return pl.pallas_call(
        body,
        out_shape=[jax.ShapeDtypeStruct((tokens, columns), kind) for kind in kinds],
        in_specs=[pl.BlockSpec(memory_space=pltpu.SMEM)] + [anywhere] * count,
        out_specs=[vmem] * len(kinds),
        scratch_shapes=[
            pltpu.VMEM((2 * len(pairs), tokens, depth), jnp.bfloat16),
            pltpu.VMEM((depth, columns), jnp.bfloat16),
            pltpu.SemaphoreType.DMA((count,)),
        ],
        compiler_params=pltpu.CompilerParams(vmem_limit_bytes=(5 + 4 * len(pairs)) << 20),
        name="partial_products",
    )(same, *acts, *weights)


def summed_over_chips(parts, sizes):
    own, across, far, far_across = parts
    groups, seqs, _ = sizes
    farthest = steered(far_across, lambda g, q, t: (groups - 1 - g, seqs - 1 - q, t), sizes)
    return (
        own,
        farthest,
        steered(far, lambda g, q, t: (groups - 1 - g, q, t), sizes),
        steered(across, lambda g, q, t: (g, seqs - 1 - q, t), sizes),
    )


def weigh(section, asked, keys, squares, cosine, sine, code, features):
    owners = len(asked)
    heads, rows, width = asked[0].shape
    tokens = code.shape[1]
    half = width // 2
    requests = 2
    factor = 1.0 / math.sqrt(width)
    span = owners * rows

    def body(section_ref, *refs):
        asked_refs, rest = refs[:owners], refs[owners:]
        key_refs = rest[:4]
        one_ref, two_ref, cos_ref, sin_ref, code_ref, weight_ref, mark_ref = rest[4:]
        scale = lax.rsqrt((one_ref[...] + two_ref[...]) / features + EPS)
        place = lax.broadcasted_iota(jnp.int32, (span, tokens), 0)
        owner = (place // rows) ^ section_ref[0]
        request = owner * requests + place % rows // (rows // requests)
        mine = request == code_ref[...]
        line = lax.broadcasted_iota(jnp.int32, (8, span), 0)
        for h in range(heads):
            columns = slice(h * width, (h + 1) * width)
            key = key_refs[0][:, columns]
            for ref in key_refs[1:]:
                key = key + ref[:, columns].astype(jnp.float32)
            first = key[:, :half]
            second = key[:, half:]
            key = jnp.concatenate(
                [
                    first * cos_ref[...] - second * sin_ref[...],
                    second * cos_ref[...] + first * sin_ref[...],
                ],
                axis=1,
            ).astype(jnp.bfloat16)
            query = jnp.concatenate([ref[h] for ref in asked_refs], axis=0)
            score = lax.dot_general(
                query, key, (((1,), (1,)), ((), ())), preferred_element_type=jnp.float32
            ) * (scale * factor)
            score = jnp.where(mine, score, NEG)
            top = jnp.max(score, axis=1, keepdims=True)
            weight = jnp.where(mine, jnp.exp(score - top), 0.0)
            total = jnp.sum(weight, axis=1, keepdims=True)
            some = total > 0.0
            safe = jnp.where(some, total, 1.0)
            weight_ref[h] = (weight / safe * scale).astype(jnp.bfloat16)
            level = jnp.where(some, top + jnp.log(safe), NEG)
            level = jnp.broadcast_to(level, (span, span)).T[:8, :]
            high = level.astype(jnp.bfloat16).astype(jnp.float32)
            middle = (level - high).astype(jnp.bfloat16).astype(jnp.float32)
            low = level - high - middle
            mark_ref[h] = jnp.where(
                line == 0, high, jnp.where(line == 1, middle, jnp.where(line == 2, low, 0.0))
            ).astype(jnp.bfloat16)

    vmem = pl.BlockSpec(memory_space=pltpu.VMEM)
    operands = (*asked, *keys, *squares, cosine, sine, code)
    return pl.pallas_call(
        body,
        out_shape=[
            jax.ShapeDtypeStruct((heads, span, tokens), jnp.bfloat16),
            jax.ShapeDtypeStruct((heads, 8, span), jnp.bfloat16),
        ],
        in_specs=[pl.BlockSpec(memory_space=pltpu.SMEM)] + [vmem] * len(operands),
        out_specs=[vmem] * 2,
        compiler_params=pltpu.CompilerParams(vmem_limit_bytes=6 << 20),
        name="weigh",
    )(section, *operands)


def mix(weights, marks, values, owners):
    heads, span, _ = weights.shape
    width = values[0].shape[1] // heads
    rows = span // owners

    def body(weight_ref, mark_ref, *rest):
        value_refs, outs = rest[: len(values)], rest[len(values) :]
        for h in range(heads):
            columns = slice(h * width, (h + 1) * width)
            value = value_refs[0][:, columns]
            for ref in value_refs[1:]:
                value = value + ref[:, columns].astype(jnp.float32)
            mixed = jnp.dot(
                weight_ref[h], value.astype(jnp.bfloat16), preferred_element_type=jnp.float32
            ).astype(jnp.bfloat16)
            for step in range(owners):
                outs[step][h, :rows, :] = mixed[step * rows : (step + 1) * rows]
                outs[step][h, rows:, :] = mark_ref[h]

    vmem = pl.BlockSpec(memory_space=pltpu.VMEM)
    operands = (weights, marks, *values)
    return pl.pallas_call(
        body,
        out_shape=[jax.ShapeDtypeStruct((heads, rows + marks.shape[1], width), jnp.bfloat16)] * owners,
        in_specs=[vmem] * len(operands),
        out_specs=[vmem] * owners,
        compiler_params=pltpu.CompilerParams(vmem_limit_bytes=4 << 20),
        name="mix",
    )(*operands)


def merge(section, pieces, mixed, levels):
    layers, spans, width = mixed.shape
    heads = pieces[0].shape[0]
    rows = spans // heads

    def body(section_ref, *rest):
        piece_refs = rest[: len(pieces)]
        mixed_ref, level_ref, out_ref = rest[len(pieces) :]
        lane = lax.broadcasted_iota(jnp.int32, (rows, width), 1)
        row = lax.broadcasted_iota(jnp.int32, (rows, width), 0)
        for step, ref in enumerate(piece_refs):
            layer = ((section_ref[0] ^ step) + 1) % layers
            routed = jnp.concatenate([ref[h, :rows, :] for h in range(heads)], axis=0)
            mine = lane == row + step * rows
            level = []
            for h in range(heads):
                marks = ref[h, rows:, :].astype(jnp.float32)
                marks = marks[0:1] + marks[1:2] + marks[2:3]
                level.append(jnp.sum(jnp.where(mine, marks, 0.0), axis=1, keepdims=True))
            level = jnp.concatenate(level, axis=0)
            high = level_ref[layer]
            peak = jnp.maximum(level, high)
            kept = jnp.exp(high - peak)
            other = jnp.exp(level - peak)
            share = 1.0 / (kept + other)
            out_ref[layer] = (
                mixed_ref[layer] * (kept * share)
                + routed.astype(jnp.float32) * (other * share)
            ).astype(jnp.bfloat16)

    vmem = pl.BlockSpec(memory_space=pltpu.VMEM)
    operands = (*pieces, mixed, levels)
    return pl.pallas_call(
        body,
        out_shape=jax.ShapeDtypeStruct((layers, spans, width), jnp.bfloat16),
        in_specs=[pl.BlockSpec(memory_space=pltpu.SMEM)] + [vmem] * len(operands),
        out_specs=vmem,
        compiler_params=pltpu.CompilerParams(vmem_limit_bytes=6 << 20),
        name="merge",
    )(section, *operands)


def keep(asked, cache, recent, lens, steps):
    layers, heads, rows, width = asked.shape
    reqs = lens.shape[0]
    filled = cache.shape[2] // reqs
    factor = 1.0 / math.sqrt(width)
    lane = (((1,), (1,)), ((), ()))

    def body(lens_ref, asked_ref, cache_ref, recent_ref, kept_ref, level_ref):
        row = lax.broadcasted_iota(jnp.int32, (rows, reqs * filled), 0)
        column = lax.broadcasted_iota(jnp.int32, (rows, reqs * filled), 1)
        own = row // (rows // reqs)
        length = lens_ref[reqs - 1]
        for r in reversed(range(reqs - 1)):
            length = jnp.where(own == r, lens_ref[r], length)
        old = (column // filled == own) & (column % filled < length)
        row = lax.broadcasted_iota(jnp.int32, (rows, reqs * steps), 0)
        column = lax.broadcasted_iota(jnp.int32, (rows, reqs * steps), 1)
        turn = row % (rows // reqs) // (rows // reqs // steps)
        new = (column // steps == row // (rows // reqs)) & (column % steps <= turn)
        for l in range(layers):
            for h in range(heads):
                query = asked_ref[l, h]
                past = cache_ref[l, h]
                step = recent_ref[l, h]
                score_old = factor * lax.dot_general(
                    query, past[:, :width], lane, preferred_element_type=jnp.float32
                )
                score_new = factor * lax.dot_general(
                    query, step[:, :width], lane, preferred_element_type=jnp.float32
                )
                score_old = jnp.where(old, score_old, NEG)
                score_new = jnp.where(new, score_new, NEG)
                top = jnp.maximum(
                    jnp.max(score_old, axis=1, keepdims=True),
                    jnp.max(score_new, axis=1, keepdims=True),
                )
                weight_old = jnp.exp(score_old - top)
                weight_new = jnp.exp(score_new - top)
                total = jnp.sum(weight_old, axis=1, keepdims=True) + jnp.sum(
                    weight_new, axis=1, keepdims=True
                )
                mixed = jnp.dot(
                    weight_old.astype(jnp.bfloat16),
                    past[:, width:],
                    preferred_element_type=jnp.float32,
                ) + jnp.dot(
                    weight_new.astype(jnp.bfloat16),
                    step[:, width:],
                    preferred_element_type=jnp.float32,
                )
                kept_ref[l, h * rows : (h + 1) * rows, :] = mixed / total
                level_ref[l, h * rows : (h + 1) * rows, :] = jnp.broadcast_to(
                    top + jnp.log(total), (rows, width)
                )

    vmem = pl.BlockSpec(memory_space=pltpu.VMEM)
    return pl.pallas_call(
        body,
        out_shape=[jax.ShapeDtypeStruct((layers, heads * rows, width), jnp.float32)] * 2,
        in_specs=[pl.BlockSpec(memory_space=pltpu.SMEM), vmem, vmem, vmem],
        out_specs=[vmem, vmem],
        compiler_params=pltpu.CompilerParams(vmem_limit_bytes=6 << 20),
        cost_estimate=pl.CostEstimate(flops=40000000000, transcendentals=0, bytes_accessed=1),
        name="keep",
    )(lens, asked, cache, recent)


def meet_local(
    handoff,
    norm_gain,
    kv_weight,
    span_start,
    token_owner,
    token_slot,
    kv_cache,
    cache_lens,
    step_kv,
    queries,
):
    sizes = (lax.axis_size("group"), lax.axis_size("seq"), lax.axis_size("tp"))
    sections = lax.axis_size("section")
    g = lax.axis_index("group")
    q = lax.axis_index("seq")
    t = lax.axis_index("tp")
    weight = kv_weight[0]
    depth = weight.shape[0] // sizes[0]
    width = weight.shape[2] // 2
    first = depth // 8
    block = handoff[0]
    tokens = block.shape[0]

    rows4 = weight.reshape(weight.shape[0], 2, 2, width).transpose(0, 2, 1, 3).reshape(-1, width)
    group = g.astype(jnp.int32)[None]
    quarter = (q * sizes[0] + g).astype(jnp.int32)[None]
    head_start, near, far = prepare(
        block,
        rows4,
        norm_gain,
        group,
        quarter,
        token_owner.reshape(1, tokens),
        token_slot,
        span_start,
        depth,
        first,
    )
    start_got = passed_along(head_start, "section", -1)

    near_got = steered(near, lambda a, b, c: (a, c, b), sizes)
    far_got = steered(far, lambda a, b, c: (sizes[0] - 1 - a, c, b), sizes)

    keys_rest, values_rest = split_heads(
        after(rows4, near), norm_gain, group, quarter, depth, first, depth - first, 7
    )
    keys_got = passed_along(keys_rest, "section", -1)
    values_got = passed_along(after(values_rest, start_got), "section", -1)

    near_mate = swapped(near_got)
    far_mate = swapped(far_got)
    same = (q == t).astype(jnp.int32)[None]

    wide = after(block, near_got).astype(jnp.float32)
    square = jnp.sum(wide * wide, axis=-1)[None]
    squares = (square, swapped(square))

    notes = start_got[first].astype(jnp.int32)
    code = notes[None, :tokens]
    begin = notes[tokens] * 64 + notes[tokens + 1]
    positions = begin + q * tokens + jnp.arange(tokens, dtype=jnp.int32)
    half = width // 2
    freq = jnp.exp(-(jnp.arange(half, dtype=jnp.float32) * 2.0 / width) * math.log(THETA))
    angle = positions.astype(jnp.float32)[:, None] * freq[None, :]
    cosine = jnp.cos(angle)
    sine = jnp.sin(angle)

    query = after(queries[0, 0], near_got)
    layers, reqs, steps, heads, flat = query.shape
    rows = reqs * steps * flat // width
    asked = query.reshape(layers, reqs, steps, heads, flat // width, width)
    asked = asked.transpose(0, 3, 1, 2, 4, 5).reshape(layers, heads, rows, width)
    section = lax.axis_index("section")
    everything = asked
    chosen = [
        lax.dynamic_index_in_dim(everything, ((section ^ n) + 1) % layers, 0, keepdims=False)
        for n in range(layers)
    ]
    cache = kv_cache[0, 0].transpose(0, 3, 1, 2, 4).reshape(layers, heads, -1, 2 * width)
    recent = step_kv[0, 0].transpose(0, 3, 1, 2, 4).reshape(layers, heads, -1, 2 * width)
    kept, levels = keep(
        everything, cache, recent, after(cache_lens[0, 0], square), steps
    )

    near_mate = after(near_mate, (cosine, sine, code, *squares, kept, levels, *chosen))
    keys_w = (start_got, keys_got)
    values_w = (start_got, values_got)
    near_pair = ((near_got,), (near_mate,))
    near_part = partial_products(same, (near_pair,), keys_w, 0, 2 * width, 0)
    far_mate = after(far_mate, near_part)
    far_pair = ((far_got,), (far_mate,))
    far_part = partial_products(same, (far_pair,), keys_w, 0, 2 * width, 2)
    keys = summed_over_chips(near_part + far_part, sizes)
    value_parts = partial_products(
        same, (near_pair, far_pair), values_w, 2 * width, 2 * width, 0
    )
    values = summed_over_chips(value_parts, sizes)
    late = after(tuple(chosen), keys[1])
    soon = after(tuple(chosen), far_part[0])
    asked = spread([soon[n] if n in (1,) else late[n] for n in range(layers)])
    features = block.shape[1] * sizes[2]
    here = section.astype(jnp.int32)[None]
    weights, marks = weigh(here, asked, keys, squares, cosine, sine, code, features)
    pieces = spread(mix(weights, marks, values, layers))
    result = merge(here, pieces, kept, levels)
    result = result.reshape(layers, heads, reqs, steps, flat // width, width)
    result = result.transpose(0, 2, 3, 1, 4, 5)
    return result.reshape(layers, reqs, steps, heads, flat)[None, None]


def solution(mesh):
    shape = mesh.shape
    paired = shape["group"] == shape["seq"] == shape["tp"] == 2
    body = meet_local if paired and shape["section"] == 4 else local
    return jax.shard_map(
        body,
        mesh=mesh,
        in_specs=(
            P(("group", "section"), "seq", "tp"),
            P("section", None),
            P("section", "seq", "tp", None),
            P(("group", "section")),
            P(("group", "section"), "seq", None),
            P(("group", "section"), "seq"),
            P(("group", "section"), "seq", None, None, None, "tp", None),
            P(("group", "section"), "seq", None),
            P(("group", "section"), "seq", None, None, None, "tp", None),
            P(("group", "section"), "seq", None, None, None, "tp", None),
        ),
        out_specs=P(("group", "section"), "seq", None, None, None, "tp", None),
        check_vma=False,
    )
```

```python
import math

import jax
import jax.numpy as jnp
from jax import lax
from jax.experimental import pallas as pl
from jax.experimental.pallas import tpu as pltpu
from jax.sharding import PartitionSpec as P

EPS = 1e-05
THETA = 500000.0
NEG = -1e30


def passed_along(value, axis, by):
    length = lax.axis_size(axis)
    return lax.ppermute(value, axis, [(i, (i + by) % length) for i in range(length)])


def rotate(pairs, positions):
    width = pairs.shape[-1] // 2
    half = width // 2
    freq = jnp.exp(-(jnp.arange(half, dtype=jnp.float32) * 2.0 / width) * math.log(THETA))
    angle = positions.astype(jnp.float32)[:, None, None] * freq[None, None, :]
    cosine = jnp.cos(angle)
    sine = jnp.sin(angle)
    first = pairs[..., :half]
    second = pairs[..., half:width]
    turned = jnp.concatenate(
        [first * cosine - second * sine, second * cosine + first * sine], axis=-1
    )
    return jnp.concatenate([turned, pairs[..., width:]], axis=-1)


def attend(query, past, lens, route_pairs, route_mask, step_pairs):
    reqs, steps, heads, flat = query.shape
    width = past.shape[-1] // 2
    groups = flat // width
    scale = 1.0 / math.sqrt(width)
    shaped = query.reshape(reqs, steps, heads, groups, width)
    score_past = (
        jnp.einsum(
            "rnhgd,rphd->rnhgp", shaped, past[..., :width], preferred_element_type=jnp.float32
        )
        * scale
    )
    score_route = (
        jnp.einsum(
            "rnhgd,khd->rnhgk", shaped, route_pairs[..., :width], preferred_element_type=jnp.float32
        )
        * scale
    )
    score_step = (
        jnp.einsum(
            "rnhgd,rmhd->rnhgm", shaped, step_pairs[..., :width], preferred_element_type=jnp.float32
        )
        * scale
    )
    past_mask = jnp.arange(past.shape[1], dtype=jnp.int32)[None, :] < lens[:, None]
    step_mask = (
        jnp.arange(steps, dtype=jnp.int32)[:, None] >= jnp.arange(steps, dtype=jnp.int32)[None, :]
    )
    score_past = jnp.where(past_mask[:, None, None, None, :], score_past, -jnp.inf)
    score_route = jnp.where(route_mask[:, None, None, None, :], score_route, -jnp.inf)
    score_step = jnp.where(step_mask[None, :, None, None, :], score_step, -jnp.inf)
    top = jnp.maximum(
        jnp.maximum(
            jnp.max(score_past, axis=-1, keepdims=True),
            jnp.max(score_route, axis=-1, keepdims=True),
        ),
        jnp.max(score_step, axis=-1, keepdims=True),
    )
    exp_past = jnp.exp(score_past - top)
    exp_route = jnp.exp(score_route - top)
    exp_step = jnp.exp(score_step - top)
    total = (
        jnp.sum(exp_past, axis=-1, keepdims=True)
        + jnp.sum(exp_route, axis=-1, keepdims=True)
        + jnp.sum(exp_step, axis=-1, keepdims=True)
    )
    w_past = (exp_past / total).astype(jnp.bfloat16)
    w_route = (exp_route / total).astype(jnp.bfloat16)
    w_step = (exp_step / total).astype(jnp.bfloat16)
    result = jnp.einsum(
        "rnhgp,rphd->rnhgd", w_past, past[..., width:], preferred_element_type=jnp.float32
    )
    result = result + jnp.einsum(
        "rnhgk,khd->rnhgd", w_route, route_pairs[..., width:], preferred_element_type=jnp.float32
    )
    result = result + jnp.einsum(
        "rnhgm,rmhd->rnhgd", w_step, step_pairs[..., width:], preferred_element_type=jnp.float32
    )
    return result.astype(jnp.bfloat16).reshape(reqs, steps, heads, flat)


def local(
    handoff,
    norm_gain,
    kv_weight,
    span_start,
    token_owner,
    token_slot,
    kv_cache,
    cache_lens,
    step_kv,
    queries,
):
    received = passed_along(handoff, "section", 1)
    whole = lax.all_gather(received[0], "tp", axis=1, tiled=True)
    tokens = whole.shape[0]
    values = whole.astype(jnp.float32)
    meansq = jnp.mean(values * values, axis=-1, keepdims=True)
    normed = (values * lax.rsqrt(meansq + EPS) * norm_gain[0][None, :]).astype(jnp.bfloat16)
    weight = kv_weight[0]
    local_heads = weight.shape[1]
    pair_width = weight.shape[2]
    columns_out = local_heads * pair_width
    piece = lax.all_gather(weight, "seq", axis=0, tiled=True)
    projected = jnp.dot(
        normed, piece.reshape(piece.shape[0], columns_out), preferred_element_type=jnp.float32
    )
    positions = span_start[0] + lax.axis_index("seq") * tokens + jnp.arange(tokens, dtype=jnp.int32)
    prompt_kv = rotate(projected.reshape(tokens, local_heads, pair_width), positions).astype(
        jnp.bfloat16
    )
    sections = lax.axis_size("section")
    capacity = 2 * tokens // sections
    owner = token_owner[0, :, 0]
    slot = token_slot[0]
    onehot = (owner[:, None] == jnp.arange(sections, dtype=jnp.int32)[None, :]).astype(jnp.bfloat16)
    lower = (
        jnp.arange(tokens, dtype=jnp.int32)[:, None] >= jnp.arange(tokens, dtype=jnp.int32)[None, :]
    ).astype(jnp.bfloat16)
    running = jnp.dot(lower, onehot, preferred_element_type=jnp.float32)
    rank = (jnp.sum(running * onehot.astype(jnp.float32), axis=1) - 1.0).astype(jnp.int32)
    place = owner * capacity + rank
    select = (place[:, None] == jnp.arange(sections * capacity, dtype=jnp.int32)[None, :]).astype(
        jnp.bfloat16
    )
    packed = jnp.einsum(
        "ts,tc->sc",
        select,
        prompt_kv.reshape(tokens, columns_out),
        preferred_element_type=jnp.float32,
    )
    packed = packed.astype(jnp.bfloat16).reshape(sections, capacity, local_heads, pair_width)
    labels = jnp.einsum(
        "ts,t->s", select, (slot + 1).astype(jnp.bfloat16), preferred_element_type=jnp.float32
    )
    labels = labels.astype(jnp.bfloat16).reshape(sections, capacity)
    routed, routed_labels = (
        lax.all_to_all(packed, "section", split_axis=0, concat_axis=0, tiled=True),
        lax.all_to_all(labels, "section", split_axis=0, concat_axis=0, tiled=True),
    )
    request_ids = (jnp.arange(kv_cache.shape[3], dtype=jnp.int32) + 1).astype(jnp.float32)
    route_mask = routed_labels.astype(jnp.float32)[:, None, :] == request_ids[None, :, None]
    layered = jax.vmap(attend, in_axes=(0, 0, None, 0, 0, 0))
    result = layered(
        queries[0, 0], kv_cache[0, 0], cache_lens[0, 0], routed, route_mask, step_kv[0, 0]
    )
    return result[None, None]


def steered(value, pairs_of, sizes):
    groups, seqs, cores = sizes
    pairs = []
    for g in range(groups):
        for q in range(seqs):
            for t in range(cores):
                a, b, c = pairs_of(g, q, t)
                pairs.append(((g * seqs + q) * cores + t, (a * seqs + b) * cores + c))
    return lax.ppermute(value, ("group", "seq", "tp"), pairs)


def swapped(value):
    return lax.ppermute(value, "tp", [(0, 1), (1, 0)])


def spread(pieces):
    return [pieces[0]] + [
        lax.ppermute(piece, "section", [(i, i ^ n) for i in range(len(pieces))])
        for n, piece in enumerate(pieces)
        if n
    ]


def after(value, early):
    return lax.optimization_barrier((value, early))[0]


def scaled_heads(wide, gain, tall, width):
    gains = jnp.concatenate(
        [
            jnp.broadcast_to(gain[:, b * width : (b + 1) * width], (width, width)).T
            for b in range(tall // width)
        ],
        axis=0,
    )
    return [
        (wide[pl.ds(n, tall, stride=4), :] * gains).astype(jnp.bfloat16) for n in range(4)
    ]


def split_heads(rows4, gain, group, quarter, depth, start, count, blocks):
    width = rows4.shape[1]
    tall = count // blocks

    def body(group_ref, quarter_ref, mixed_ref, gain_ref, key_ref, value_ref, wide):
        wide[...] = mixed_ref[...].astype(jnp.float32)
        parts = scaled_heads(wide, gain_ref[...], tall, width)
        for head in range(2):
            key_ref[:, head * width : (head + 1) * width] = parts[head]
            value_ref[:, head * width : (head + 1) * width] = parts[2 + head]

    return pl.pallas_call(
        body,
        out_shape=[jax.ShapeDtypeStruct((count, 2 * width), jnp.bfloat16)] * 2,
        grid_spec=pltpu.PrefetchScalarGridSpec(
            num_scalar_prefetch=2,
            grid=(blocks,),
            in_specs=[
                pl.BlockSpec(
                    (4 * tall, width),
                    lambda i, group, quarter: (group[0] * (depth // tall) + start // tall + i, 0),
                ),
                pl.BlockSpec(
                    (1, tall),
                    lambda i, group, quarter: (0, quarter[0] * (depth // tall) + start // tall + i),
                ),
            ],
            out_specs=[pl.BlockSpec((tall, 2 * width), lambda i, group, quarter: (i, 0))] * 2,
            scratch_shapes=[pltpu.VMEM((4 * tall, width), jnp.float32)],
        ),
        compiler_params=pltpu.CompilerParams(vmem_limit_bytes=57 << 20),
        name="split_heads",
    )(group, quarter, rows4, gain)


def prepare(block, rows4, gain, owner, slot, begin, depth, first):
    tokens = block.shape[0]
    width = rows4.shape[1]
    extra = 16
    halves = 2
    piece = tokens // halves

    def body(
        owner_ref,
        slot_ref,
        begin_ref,
        block_ref,
        rows_ref,
        gain_ref,
        head_ref,
        near_ref,
        far_ref,
        mixed,
        wide,
        gains,
        held,
        head,
        owners,
        slots,
        start_at,
        sems,
    ):
        group = lax.axis_index("group")
        quarter = lax.axis_index("seq") * lax.axis_size("group") + group
        row = pl.multiple_of(group * (4 * depth), 4 * depth)
        lane = pl.multiple_of(quarter * depth, depth)
        small = [
            pltpu.make_async_copy(rows_ref.at[pl.ds(row, 4 * first), :], mixed, sems.at[0]),
            pltpu.make_async_copy(gain_ref.at[:, pl.ds(lane, first)], gains, sems.at[1]),
            pltpu.make_async_copy(owner_ref, owners, sems.at[2]),
            pltpu.make_async_copy(slot_ref, slots, sems.at[3]),
            pltpu.make_async_copy(begin_ref, start_at, sems.at[4]),
        ]
        loads = []
        stores = []
        for n, ref in enumerate((near_ref, far_ref)):
            which = group if n == 0 else 1 - group
            column = pl.multiple_of(which * depth, depth)
            for k in range(halves):
                part = pl.ds(k * piece, piece)
                at = 6 + 2 * (halves * n + k)
                loads.append(
                    pltpu.make_async_copy(
                        block_ref.at[part, pl.ds(column, depth)], held.at[n, part], sems.at[at]
                    )
                )
                stores.append(
                    pltpu.make_async_copy(held.at[n, part], ref.at[part, :], sems.at[at + 1])
                )
        for copy in small + loads:
            copy.start()
        for load, store in zip(loads, stores):
            load.wait()
            store.start()
        for copy in small:
            copy.wait()
        wide[...] = mixed[...].astype(jnp.float32)
        for n, part in enumerate(scaled_heads(wide, gains[...], first, width)):
            head[:first, n * width : (n + 1) * width] = part
        code = (owners[...] * 2 + slots[...]).astype(jnp.float32)
        start = start_at[0]
        high = start // 64
        mark = lax.broadcasted_iota(jnp.int32, (1, 4 * width - tokens), 1)
        mark = jnp.where(mark == 0, high, jnp.where(mark == 1, start - high * 64, 0))
        head[first:, :tokens] = jnp.broadcast_to(code, (extra, tokens)).astype(jnp.bfloat16)
        head[first:, tokens:] = jnp.broadcast_to(
            mark.astype(jnp.float32), (extra, 4 * width - tokens)
        ).astype(jnp.bfloat16)
        stores.append(pltpu.make_async_copy(head, head_ref, sems.at[5]))
        stores[-1].start()
        for store in stores:
            store.wait()

    anywhere = pl.BlockSpec(memory_space=pl.ANY)
    return pl.pallas_call(
        body,
        out_shape=[jax.ShapeDtypeStruct((first + extra, 4 * width), jnp.bfloat16)]
        + [jax.ShapeDtypeStruct((tokens, depth), jnp.bfloat16)] * 2,
        in_specs=[anywhere] * 6,
        out_specs=[anywhere] * 3,
        scratch_shapes=[
            pltpu.VMEM((4 * first, width), jnp.bfloat16),
            pltpu.VMEM((4 * first, width), jnp.float32),
            pltpu.VMEM((1, first), jnp.float32),
            pltpu.VMEM((2, tokens, depth), jnp.bfloat16),
            pltpu.VMEM((first + extra, 4 * width), jnp.bfloat16),
            pltpu.VMEM((1, tokens), jnp.int32),
            pltpu.VMEM((1, tokens), jnp.int32),
            pltpu.SMEM((1,), jnp.int32),
            pltpu.SemaphoreType.DMA((6 + 4 * halves,)),
        ],
        compiler_params=pltpu.CompilerParams(vmem_limit_bytes=60 << 20),
        name="prepare",
    )(owner, slot, begin, block, rows4, gain)


def partial_products(same, pairs, weights, first_column, columns, first_kind):
    tokens = pairs[0][0][0].shape[0]
    depth = pairs[0][0][0].shape[1]
    acts = [piece for pair in pairs for side in pair for piece in side]
    count = len(acts) + len(weights)

    def body(same_ref, *refs):
        act_refs = refs[: len(acts)]
        weight_refs = refs[len(acts) : count]
        outs = refs[count : count + 2 * len(pairs)]
        held, weight, sems = refs[count + 2 * len(pairs) :]
        weight_copies = []
        row = 0
        for n, ref in enumerate(weight_refs):
            taken = min(ref.shape[0], depth - row) // 128 * 128
            column = first_column if ref.shape[1] > columns else 0
            weight_copies.append(
                pltpu.make_async_copy(
                    ref.at[pl.ds(0, taken), pl.ds(column, columns)],
                    weight.at[pl.ds(row, taken), :],
                    sems.at[len(acts) + n],
                )
            )
            row += taken
        for copy in weight_copies:
            copy.start()
        act_copies = []
        n = 0
        for p, pair in enumerate(pairs):
            mine = []
            for side in range(2):
                slot = 2 * p + ((1 - same_ref[0]) if side == 0 else same_ref[0])
                column = 0
                for piece in pair[side]:
                    wide = piece.shape[1]
                    copy = pltpu.make_async_copy(
                        act_refs[n], held.at[slot, :, pl.ds(column, wide)], sems.at[n]
                    )
                    copy.start()
                    mine.append(copy)
                    column += wide
                    n += 1
            act_copies.append(mine)
        for copy in weight_copies:
            copy.wait()
        for p in range(len(pairs)):
            for copy in act_copies[p]:
                copy.wait()
            for side in range(2):
                out = outs[2 * p + side]
                out[...] = jnp.dot(
                    held[2 * p + side], weight[...], preferred_element_type=jnp.float32
                ).astype(out.dtype)

    anywhere = pl.BlockSpec(memory_space=pl.ANY)
    vmem = pl.BlockSpec(memory_space=pltpu.VMEM)
    kinds = [jnp.float32, jnp.bfloat16, jnp.bfloat16, jnp.bfloat16]
    kinds = kinds[first_kind : first_kind + 2 * len(pairs)]
    return pl.pallas_call(
        body,
        out_shape=[jax.ShapeDtypeStruct((tokens, columns), kind) for kind in kinds],
        in_specs=[pl.BlockSpec(memory_space=pltpu.SMEM)] + [anywhere] * count,
        out_specs=[vmem] * len(kinds),
        scratch_shapes=[
            pltpu.VMEM((2 * len(pairs), tokens, depth), jnp.bfloat16),
            pltpu.VMEM((depth, columns), jnp.bfloat16),
            pltpu.SemaphoreType.DMA((count,)),
        ],
        compiler_params=pltpu.CompilerParams(vmem_limit_bytes=(5 + 4 * len(pairs)) << 20),
        name="partial_products",
    )(same, *acts, *weights)


def summed_over_chips(parts, sizes):
    own, across, far, far_across = parts
    groups, seqs, _ = sizes
    farthest = steered(far_across, lambda g, q, t: (groups - 1 - g, seqs - 1 - q, t), sizes)
    return (
        own,
        farthest,
        steered(far, lambda g, q, t: (groups - 1 - g, q, t), sizes),
        steered(across, lambda g, q, t: (g, seqs - 1 - q, t), sizes),
    )


def weigh(section, asked, keys, squares, cosine, sine, code, features):
    owners = len(asked)
    heads, rows, width = asked[0].shape
    tokens = code.shape[1]
    half = width // 2
    requests = 2
    factor = 1.0 / math.sqrt(width)
    span = owners * rows

    def body(section_ref, *refs):
        asked_refs, rest = refs[:owners], refs[owners:]
        key_refs = rest[:4]
        one_ref, two_ref, cos_ref, sin_ref, code_ref, weight_ref, mark_ref = rest[4:]
        scale = lax.rsqrt((one_ref[...] + two_ref[...]) / features + EPS)
        place = lax.broadcasted_iota(jnp.int32, (span, tokens), 0)
        owner = (place // rows) ^ section_ref[0]
        request = owner * requests + place % rows // (rows // requests)
        mine = request == code_ref[...]
        line = lax.broadcasted_iota(jnp.int32, (8, span), 0)
        for h in range(heads):
            columns = slice(h * width, (h + 1) * width)
            key = key_refs[0][:, columns]
            for ref in key_refs[1:]:
                key = key + ref[:, columns].astype(jnp.float32)
            first = key[:, :half]
            second = key[:, half:]
            key = jnp.concatenate(
                [
                    first * cos_ref[...] - second * sin_ref[...],
                    second * cos_ref[...] + first * sin_ref[...],
                ],
                axis=1,
            ).astype(jnp.bfloat16)
            query = jnp.concatenate([ref[h] for ref in asked_refs], axis=0)
            score = lax.dot_general(
                query, key, (((1,), (1,)), ((), ())), preferred_element_type=jnp.float32
            ) * (scale * factor)
            score = jnp.where(mine, score, NEG)
            top = jnp.max(score, axis=1, keepdims=True)
            weight = jnp.where(mine, jnp.exp(score - top), 0.0)
            total = jnp.sum(weight, axis=1, keepdims=True)
            some = total > 0.0
            safe = jnp.where(some, total, 1.0)
            weight_ref[h] = (weight / safe * scale).astype(jnp.bfloat16)
            level = jnp.where(some, top + jnp.log(safe), NEG)
            level = jnp.broadcast_to(level, (span, span)).T[:8, :]
            high = level.astype(jnp.bfloat16).astype(jnp.float32)
            middle = (level - high).astype(jnp.bfloat16).astype(jnp.float32)
            low = level - high - middle
            mark_ref[h] = jnp.where(
                line == 0, high, jnp.where(line == 1, middle, jnp.where(line == 2, low, 0.0))
            ).astype(jnp.bfloat16)

    vmem = pl.BlockSpec(memory_space=pltpu.VMEM)
    operands = (*asked, *keys, *squares, cosine, sine, code)
    return pl.pallas_call(
        body,
        out_shape=[
            jax.ShapeDtypeStruct((heads, span, tokens), jnp.bfloat16),
            jax.ShapeDtypeStruct((heads, 8, span), jnp.bfloat16),
        ],
        in_specs=[pl.BlockSpec(memory_space=pltpu.SMEM)] + [vmem] * len(operands),
        out_specs=[vmem] * 2,
        compiler_params=pltpu.CompilerParams(vmem_limit_bytes=6 << 20),
        name="weigh",
    )(section, *operands)


def mix(weights, marks, values, owners):
    heads, span, _ = weights.shape
    width = values[0].shape[1] // heads
    rows = span // owners

    def body(weight_ref, mark_ref, *rest):
        value_refs, outs = rest[: len(values)], rest[len(values) :]
        for h in range(heads):
            columns = slice(h * width, (h + 1) * width)
            value = value_refs[0][:, columns]
            for ref in value_refs[1:]:
                value = value + ref[:, columns].astype(jnp.float32)
            mixed = jnp.dot(
                weight_ref[h], value.astype(jnp.bfloat16), preferred_element_type=jnp.float32
            ).astype(jnp.bfloat16)
            for step in range(owners):
                outs[step][h, :rows, :] = mixed[step * rows : (step + 1) * rows]
                outs[step][h, rows:, :] = mark_ref[h]

    vmem = pl.BlockSpec(memory_space=pltpu.VMEM)
    operands = (weights, marks, *values)
    return pl.pallas_call(
        body,
        out_shape=[jax.ShapeDtypeStruct((heads, rows + marks.shape[1], width), jnp.bfloat16)] * owners,
        in_specs=[vmem] * len(operands),
        out_specs=[vmem] * owners,
        compiler_params=pltpu.CompilerParams(vmem_limit_bytes=4 << 20),
        name="mix",
    )(*operands)


def merge(section, pieces, mixed, levels):
    layers, spans, width = mixed.shape
    heads = pieces[0].shape[0]
    rows = spans // heads

    def body(section_ref, *rest):
        piece_refs = rest[: len(pieces)]
        mixed_ref, level_ref, out_ref = rest[len(pieces) :]
        lane = lax.broadcasted_iota(jnp.int32, (rows, width), 1)
        row = lax.broadcasted_iota(jnp.int32, (rows, width), 0)
        for step, ref in enumerate(piece_refs):
            layer = ((section_ref[0] ^ step) + 1) % layers
            routed = jnp.concatenate([ref[h, :rows, :] for h in range(heads)], axis=0)
            mine = lane == row + step * rows
            level = []
            for h in range(heads):
                marks = ref[h, rows:, :].astype(jnp.float32)
                marks = marks[0:1] + marks[1:2] + marks[2:3]
                level.append(jnp.sum(jnp.where(mine, marks, 0.0), axis=1, keepdims=True))
            level = jnp.concatenate(level, axis=0)
            high = level_ref[layer]
            peak = jnp.maximum(level, high)
            kept = jnp.exp(high - peak)
            other = jnp.exp(level - peak)
            share = 1.0 / (kept + other)
            out_ref[layer] = (
                mixed_ref[layer] * (kept * share)
                + routed.astype(jnp.float32) * (other * share)
            ).astype(jnp.bfloat16)

    vmem = pl.BlockSpec(memory_space=pltpu.VMEM)
    operands = (*pieces, mixed, levels)
    return pl.pallas_call(
        body,
        out_shape=jax.ShapeDtypeStruct((layers, spans, width), jnp.bfloat16),
        in_specs=[pl.BlockSpec(memory_space=pltpu.SMEM)] + [vmem] * len(operands),
        out_specs=vmem,
        compiler_params=pltpu.CompilerParams(vmem_limit_bytes=6 << 20),
        name="merge",
    )(section, *operands)


def keep(asked, cache, recent, lens, steps):
    layers, heads, rows, width = asked.shape
    reqs = lens.shape[0]
    filled = cache.shape[2] // reqs
    factor = 1.0 / math.sqrt(width)
    lane = (((1,), (1,)), ((), ()))

    def body(lens_ref, asked_ref, cache_ref, recent_ref, kept_ref, level_ref):
        row = lax.broadcasted_iota(jnp.int32, (rows, reqs * filled), 0)
        column = lax.broadcasted_iota(jnp.int32, (rows, reqs * filled), 1)
        own = row // (rows // reqs)
        length = lens_ref[reqs - 1]
        for r in reversed(range(reqs - 1)):
            length = jnp.where(own == r, lens_ref[r], length)
        old = (column // filled == own) & (column % filled < length)
        row = lax.broadcasted_iota(jnp.int32, (rows, reqs * steps), 0)
        column = lax.broadcasted_iota(jnp.int32, (rows, reqs * steps), 1)
        turn = row % (rows // reqs) // (rows // reqs // steps)
        new = (column // steps == row // (rows // reqs)) & (column % steps <= turn)
        for l in range(layers):
            for h in range(heads):
                query = asked_ref[l, h]
                past = cache_ref[l, h]
                step = recent_ref[l, h]
                score_old = factor * lax.dot_general(
                    query, past[:, :width], lane, preferred_element_type=jnp.float32
                )
                score_new = factor * lax.dot_general(
                    query, step[:, :width], lane, preferred_element_type=jnp.float32
                )
                score_old = jnp.where(old, score_old, NEG)
                score_new = jnp.where(new, score_new, NEG)
                top = jnp.maximum(
                    jnp.max(score_old, axis=1, keepdims=True),
                    jnp.max(score_new, axis=1, keepdims=True),
                )
                weight_old = jnp.exp(score_old - top)
                weight_new = jnp.exp(score_new - top)
                total = jnp.sum(weight_old, axis=1, keepdims=True) + jnp.sum(
                    weight_new, axis=1, keepdims=True
                )
                mixed = jnp.dot(
                    weight_old.astype(jnp.bfloat16),
                    past[:, width:],
                    preferred_element_type=jnp.float32,
                ) + jnp.dot(
                    weight_new.astype(jnp.bfloat16),
                    step[:, width:],
                    preferred_element_type=jnp.float32,
                )
                kept_ref[l, h * rows : (h + 1) * rows, :] = mixed / total
                level_ref[l, h * rows : (h + 1) * rows, :] = jnp.broadcast_to(
                    top + jnp.log(total), (rows, width)
                )

    vmem = pl.BlockSpec(memory_space=pltpu.VMEM)
    return pl.pallas_call(
        body,
        out_shape=[jax.ShapeDtypeStruct((layers, heads * rows, width), jnp.float32)] * 2,
        in_specs=[pl.BlockSpec(memory_space=pltpu.SMEM), vmem, vmem, vmem],
        out_specs=[vmem, vmem],
        compiler_params=pltpu.CompilerParams(vmem_limit_bytes=6 << 20),
        cost_estimate=pl.CostEstimate(flops=40000000000, transcendentals=0, bytes_accessed=1),
        name="keep",
    )(lens, asked, cache, recent)


def meet_local(
    handoff,
    norm_gain,
    kv_weight,
    span_start,
    token_owner,
    token_slot,
    kv_cache,
    cache_lens,
    step_kv,
    queries,
):
    sizes = (lax.axis_size("group"), lax.axis_size("seq"), lax.axis_size("tp"))
    sections = lax.axis_size("section")
    g = lax.axis_index("group")
    q = lax.axis_index("seq")
    t = lax.axis_index("tp")
    weight = kv_weight[0]
    depth = weight.shape[0] // sizes[0]
    width = weight.shape[2] // 2
    first = depth // 8
    block = handoff[0]
    tokens = block.shape[0]

    rows4 = weight.reshape(weight.shape[0], 2, 2, width).transpose(0, 2, 1, 3).reshape(-1, width)
    group = g.astype(jnp.int32)[None]
    quarter = (q * sizes[0] + g).astype(jnp.int32)[None]
    head_start, near, far = prepare(
        block,
        rows4,
        norm_gain,
        token_owner.reshape(1, tokens),
        token_slot,
        span_start,
        depth,
        first,
    )
    start_got = passed_along(head_start, "section", -1)

    near_got = steered(near, lambda a, b, c: (a, c, b), sizes)
    far_got = steered(far, lambda a, b, c: (sizes[0] - 1 - a, c, b), sizes)

    keys_rest, values_rest = split_heads(
        after(rows4, near), norm_gain, group, quarter, depth, first, depth - first, 7
    )
    keys_got = passed_along(keys_rest, "section", -1)
    values_got = passed_along(after(values_rest, start_got), "section", -1)

    near_mate = swapped(near_got)
    far_mate = swapped(far_got)
    same = (q == t).astype(jnp.int32)[None]

    wide = after(block, near_got).astype(jnp.float32)
    square = jnp.sum(wide * wide, axis=-1)[None]
    squares = (square, swapped(square))

    notes = start_got[first].astype(jnp.int32)
    code = notes[None, :tokens]
    begin = notes[tokens] * 64 + notes[tokens + 1]
    positions = begin + q * tokens + jnp.arange(tokens, dtype=jnp.int32)
    half = width // 2
    freq = jnp.exp(-(jnp.arange(half, dtype=jnp.float32) * 2.0 / width) * math.log(THETA))
    angle = positions.astype(jnp.float32)[:, None] * freq[None, :]
    cosine = jnp.cos(angle)
    sine = jnp.sin(angle)

    query = after(queries[0, 0], near_got)
    layers, reqs, steps, heads, flat = query.shape
    rows = reqs * steps * flat // width
    asked = query.reshape(layers, reqs, steps, heads, flat // width, width)
    asked = asked.transpose(0, 3, 1, 2, 4, 5).reshape(layers, heads, rows, width)
    section = lax.axis_index("section")
    everything = asked
    chosen = [
        lax.dynamic_index_in_dim(everything, ((section ^ n) + 1) % layers, 0, keepdims=False)
        for n in range(layers)
    ]
    cache = kv_cache[0, 0].transpose(0, 3, 1, 2, 4).reshape(layers, heads, -1, 2 * width)
    recent = step_kv[0, 0].transpose(0, 3, 1, 2, 4).reshape(layers, heads, -1, 2 * width)
    kept, levels = keep(
        everything, cache, recent, after(cache_lens[0, 0], square), steps
    )

    near_mate = after(near_mate, (cosine, sine, code, *squares, kept, levels, *chosen))
    keys_w = (start_got, keys_got)
    values_w = (start_got, values_got)
    near_pair = ((near_got,), (near_mate,))
    near_part = partial_products(same, (near_pair,), keys_w, 0, 2 * width, 0)
    far_mate = after(far_mate, near_part)
    far_pair = ((far_got,), (far_mate,))
    far_part = partial_products(same, (far_pair,), keys_w, 0, 2 * width, 2)
    keys = summed_over_chips(near_part + far_part, sizes)
    value_parts = partial_products(
        same, (near_pair, far_pair), values_w, 2 * width, 2 * width, 0
    )
    values = summed_over_chips(value_parts, sizes)
    late = after(tuple(chosen), keys[1])
    soon = after(tuple(chosen), far_part[0])
    asked = spread([soon[n] if n in (1,) else late[n] for n in range(layers)])
    features = block.shape[1] * sizes[2]
    here = section.astype(jnp.int32)[None]
    weights, marks = weigh(here, asked, keys, squares, cosine, sine, code, features)
    pieces = spread(mix(weights, marks, values, layers))
    result = merge(here, pieces, kept, levels)
    result = result.reshape(layers, heads, reqs, steps, flat // width, width)
    result = result.transpose(0, 2, 3, 1, 4, 5)
    return result.reshape(layers, reqs, steps, heads, flat)[None, None]


def solution(mesh):
    shape = mesh.shape
    paired = shape["group"] == shape["seq"] == shape["tp"] == 2
    body = meet_local if paired and shape["section"] == 4 else local
    return jax.shard_map(
        body,
        mesh=mesh,
        in_specs=(
            P(("group", "section"), "seq", "tp"),
            P("section", None),
            P("section", "seq", "tp", None),
            P(("group", "section")),
            P(("group", "section"), "seq", None),
            P(("group", "section"), "seq"),
            P(("group", "section"), "seq", None, None, None, "tp", None),
            P(("group", "section"), "seq", None),
            P(("group", "section"), "seq", None, None, None, "tp", None),
            P(("group", "section"), "seq", None, None, None, "tp", None),
        ),
        out_specs=P(("group", "section"), "seq", None, None, None, "tp", None),
        check_vma=False,
    )
```
